32 devices in a mesh: dp: 8 (over z, x), tm: 4 (over y, core).
Axes of the slice: x: 2, y: 2, z: 4, core: 2. Of those that a mesh axis runs over, the one named last changes fastest.
Arguments:
- frames: bfloat16 [8, 512, 1536], P('dp', 'tm'), may hold values from -3 to 3
- query: bfloat16 [8, 512, 1536], P('dp', 'tm'), may hold values from -6 to 6
- keys: bfloat16 [8, 512, 1536], P('dp', 'tm'), may hold values from -6 to 6
- values: bfloat16 [8, 512, 1536], P('dp', 'tm'), may hold values from -6 to 6
- norm_gain: float32 [1536], replicated, may hold values from 0.1 to 1.9
- conv_gain: float32 [1536], replicated, may hold values from 0.1 to 1.9
- w_glu: bfloat16 [1536, 3072], P('tm'), may hold values from -0.15625 to 0.15625
- taps: float32 [32, 1536], replicated, may hold values from -1 to 1
- w_out: bfloat16 [1536, 1536], P('tm'), may hold values from -0.15625 to 0.15625
- cotangent: bfloat16 [8, 512, 1536], P('dp', 'tm'), may hold values from -0.09375 to 0.09375
Outputs:
- glu_grad: float32 [1536, 3072], P('tm')
- taps_grad: float32 [32, 1536], P(None, 'tm')
- out_grad: float32 [1536, 1536], P('tm')
The draws below stay inside these ranges and needn't reach their ends.
All inputs are finite; a program needn't handle non-finite values.
Results may differ from the reference program's by a relative error of at most 0.02.
Values may be sent and summed in bfloat16 or wider, within the bound.
No kernel may reach another device: no remote copies, remote signals or barrier semaphores. Data moves between devices by JAX's collectives and lax.ppermute only.
A program may use at most 128 MiB of HBM per device.

```python
import jax
import jax.numpy as jnp
from jax import lax

D = 1536
HEADS = 16
FF2 = 3072
KERNEL = 32
TOK_DEV = 128
HEAD_DIM = 96
LENGTH = 512
SEQS = 8
N_TM = 4


def drawn_pair(key):
    base = jax.random.fold_in(key, 11)
    first, second = jax.random.split(base, 2)
    shape = (SEQS, LENGTH, D)
    query = jnp.clip(jax.random.normal(first, shape, jnp.float32), -6.0, 6.0)
    keys = jnp.clip(2.0 * jax.random.normal(second, shape, jnp.float32), -6.0, 6.0)
    return (query, keys)


def draw_query(key, part):
    return drawn_pair(key)[0].astype(jnp.bfloat16)


def draw_keys(key, part):
    return drawn_pair(key)[1].astype(jnp.bfloat16)


def block_levels(key, extent, shards, smallest, largest):
    gain = 1.0
    for dim, parts in shards:
        steps = jax.random.uniform(jax.random.fold_in(jax.random.fold_in(key, 6), dim), (parts,), jnp.float32, smallest / len(shards), largest / len(shards))
        gain = gain * jnp.repeat(jnp.exp(steps), extent[dim] // parts).reshape((-1,) + (1,) * (len(extent) - 1 - dim))
    return gain


def noise(key, extent, spread, limit, shards=(), held_as=jnp.bfloat16):
    values = jax.random.normal(key, extent, jnp.float32) * spread
    if len(shards) > 0:
        values = block_levels(key, extent, shards, -0.22, 0.18) * values
    return jnp.clip(values, min=-limit, max=limit).astype(held_as)


def setup_inputs(seed: int = 0) -> dict:
    splits = jax.random.split(jax.random.key(seed), 11)
    frames = noise(splits[0], (SEQS, LENGTH, D), 0.5, 3.0, ((0, 8), (1, 4)))
    query = draw_query(jax.random.fold_in(splits[10], 71), 0)
    keys = draw_keys(jax.random.fold_in(splits[10], 71), 0)
    values = noise(splits[3], (SEQS, LENGTH, D), 1.0, 6.0, ((0, 8), (1, 4)))
    norm_gain = jnp.clip(1.0 + 0.18 * jax.random.normal(splits[4], (D,), jnp.float32), 0.1, 1.9)
    conv_gain = jnp.clip(1.0 + 0.18 * jax.random.normal(splits[5], (D,), jnp.float32), 0.1, 1.9)
    w_glu = noise(splits[6], (D, FF2), D ** -0.5, 0.15625, ((0, 4),))
    taps = noise(splits[7], (KERNEL, D), KERNEL ** -0.5, 1.0, (), jnp.float32)
    w_out = noise(splits[8], (D, D), D ** -0.5, 0.15625, ((0, 4),))
    cotangent = noise(splits[9], (SEQS, LENGTH, D), (SEQS * LENGTH) ** -0.5, 0.09375, ((0, 8), (1, 4)))
    return {"frames": frames, "query": query, "keys": keys, "values": values, "norm_gain": norm_gain, "conv_gain": conv_gain, "w_glu": w_glu, "taps": taps, "w_out": w_out, "cotangent": cotangent}


def standard(v):
    mean = lax.optimization_barrier(jnp.mean(v, axis=-1, keepdims=True))
    centred = v - mean
    var = lax.optimization_barrier(jnp.mean(centred * centred, axis=-1, keepdims=True))
    inv = lax.rsqrt(var + 1e-05)
    return (centred * inv, inv)

def attend(query, keys, values):
    length = query.shape[0]
    stacked = jnp.stack([query, keys, values]).reshape(3, length, HEADS, HEAD_DIM)
    stacked = stacked.transpose(2, 0, 1, 3)

    def one_head(trio):
        scores = jnp.dot(trio[0], trio[1].T, preferred_element_type=jnp.float32) * HEAD_DIM ** (-0.5)
        top = lax.optimization_barrier(jnp.max(scores, axis=1, keepdims=True))
        expo = jnp.exp(scores - top)
        total = lax.optimization_barrier(jnp.sum(expo, axis=1, keepdims=True))
        weights = expo.astype(jnp.bfloat16)
        return (jnp.dot(weights, trio[2], preferred_element_type=jnp.float32) / total).astype(jnp.bfloat16)
    heads_out = lax.map(one_head, stacked)
    return heads_out.transpose(1, 0, 2).reshape(length, D)

def rounded(value):
    return lax.optimization_barrier(value.astype(jnp.bfloat16)).astype(jnp.float32)

def utterance(carry, inputs, norm_gain, conv_gain, w_glu, taps, w_out):
    frames, query, keys, values, cotangent = inputs
    half = KERNEL // 2
    attention = attend(query, keys, values)
    mixed = frames.astype(jnp.float32) + attention.astype(jnp.float32)
    normed, unused = standard(mixed)
    u_rows = (normed * norm_gain).astype(jnp.bfloat16)
    p_full = jnp.dot(u_rows, w_glu, preferred_element_type=jnp.float32)
    first = p_full[:, :D]
    sig = jax.nn.sigmoid(p_full[:, D:])
    y_rows = (first * sig).astype(jnp.bfloat16)
    padded = jnp.pad(y_rows, ((half, half), (0, 0)))
    z_rows = jnp.zeros((LENGTH, D), jnp.float32)
    for k in range(KERNEL):
        z_rows = z_rows + taps[k] * padded[k:k + LENGTH].astype(jnp.float32)
    zhat, inv = standard(z_rows)
    n_rows = zhat * conv_gain
    sgate = jax.nn.sigmoid(n_rows)
    s_rows = (n_rows * sgate).astype(jnp.bfloat16)
    d_s = jnp.dot(cotangent, w_out.T, preferred_element_type=jnp.float32)
    d_n = d_s * sgate * (1.0 + n_rows * (1.0 - sgate))
    e_rows = d_n * conv_gain
    d_z = ((e_rows - lax.optimization_barrier(jnp.mean(e_rows, axis=-1, keepdims=True)) - zhat * lax.optimization_barrier(jnp.mean(e_rows * zhat, axis=-1, keepdims=True))) * inv).astype(jnp.bfloat16)
    dz_pad = jnp.pad(d_z, ((half, half), (0, 0)))
    d_y = jnp.zeros((LENGTH, D), jnp.float32)
    for k in range(KERNEL):
        d_y = d_y + taps[k] * dz_pad[2 * half - k:2 * half - k + LENGTH].astype(jnp.float32)
    d_p = jnp.concatenate([d_y * sig, d_y * first * sig * (1.0 - sig)], axis=1).astype(jnp.bfloat16)

    def block(totals, index):
        start = (index * TOK_DEV).astype(jnp.int32)
        u_b = lax.dynamic_slice_in_dim(u_rows, start, TOK_DEV, 0)
        p_b = lax.dynamic_slice_in_dim(d_p, start, TOK_DEV, 0)
        s_b = lax.dynamic_slice_in_dim(s_rows, start, TOK_DEV, 0)
        c_b = lax.dynamic_slice_in_dim(cotangent, start, TOK_DEV, 0)
        z_b = lax.dynamic_slice_in_dim(d_z, start, TOK_DEV, 0).astype(jnp.float32)
        glu_part = jnp.dot(u_b.T, p_b, preferred_element_type=jnp.float32)
        out_part = jnp.dot(s_b.T, c_b, preferred_element_type=jnp.float32)
        taps_part = jnp.stack([lax.optimization_barrier(jnp.sum(z_b * lax.dynamic_slice_in_dim(padded, start + k, TOK_DEV, 0).astype(jnp.float32), axis=0)) for k in range(KERNEL)])
        return ((totals[0] + rounded(glu_part), totals[1] + rounded(taps_part), totals[2] + rounded(out_part)), None)
    carry, unused_out = lax.scan(block, carry, jnp.arange(N_TM, dtype=jnp.int32))
    return (carry, None)

def reference(frames, query, keys, values, norm_gain, conv_gain, w_glu, taps, w_out, cotangent):
    start_sums = (jnp.zeros((D, FF2), jnp.float32), jnp.zeros((KERNEL, D), jnp.float32), jnp.zeros((D, D), jnp.float32))

    def step(carry, inputs):
        return utterance(carry, inputs, norm_gain, conv_gain, w_glu, taps, w_out)
    sums, unused = lax.scan(step, start_sums, (frames, query, keys, values, cotangent))
    return (sums[0], sums[1], sums[2])
```

```python
import jax
import jax.numpy as jnp
from jax import lax
from jax.sharding import PartitionSpec as P

HEADS = 16
F32 = jnp.float32
BF16 = jnp.bfloat16


def bits_of(axis):
    size = lax.axis_size(axis)
    return [1 << i for i in range(size.bit_length() - 1)]


def swap(value, axis, offset):
    size = lax.axis_size(axis)
    return lax.ppermute(value, axis, [(i, i ^ offset) for i in range(size)])


def to_channels(arr):
    groups = lax.axis_size("tm")
    count, rows, width = arr.shape
    block = width // groups
    split = arr.reshape(count, rows, groups, block).transpose(2, 0, 1, 3)
    moved = lax.all_to_all(split, "tm", split_axis=0, concat_axis=0, tiled=True)
    return [moved[:, i].reshape(groups * rows, block) for i in range(count)]


def attend(query, keys, values, head_dim):
    length, width = query.shape
    shape = (length, width // head_dim, head_dim)
    q, k, v = query.reshape(shape), keys.reshape(shape), values.reshape(shape)
    scores = jnp.einsum("qhd,khd->hqk", q, k, preferred_element_type=F32) * head_dim ** (-0.5)
    top = jnp.max(scores, axis=2, keepdims=True)
    expo = jnp.exp(scores - top)
    total = jnp.sum(expo, axis=2)
    summed = jnp.einsum("hqk,khd->qhd", expo.astype(BF16), v, preferred_element_type=F32)
    return (summed / total.T[:, :, None]).astype(BF16).reshape(length, width)


def moments(value):
    count = value.shape[1]
    mean = jnp.mean(value, axis=1)
    centred = value - mean[:, None]
    spread = jnp.sum(centred * centred, axis=1)
    for bit in bits_of("tm"):
        other = swap(jnp.stack([mean, spread]), "tm", bit)
        gap = mean - other[0]
        spread = spread + other[1] + gap * gap * (0.5 * count)
        mean = 0.5 * (mean + other[0])
        count = 2 * count
    return mean[:, None], lax.rsqrt(spread / count + 1e-05)[:, None]


def row_means(first, second):
    count = first.shape[1] * lax.axis_size("tm")
    sums = jnp.stack([jnp.sum(first, axis=1), jnp.sum(second, axis=1)])
    for bit in bits_of("tm"):
        sums = sums + swap(sums, "tm", bit)
    sums = sums / count
    return sums[0][:, None], sums[1][:, None]


def gather_rows(value, axis, order):
    index = lax.axis_index(axis)
    value = value[(None,) * len(order)]
    for bit in order:
        other = swap(value, axis, bit)
        upper = (index // bit) % 2 == 1
        place = len(order) - bit.bit_length()
        value = jnp.concatenate(
            [jnp.where(upper, other, value), jnp.where(upper, value, other)], axis=place
        )
    return value.reshape((lax.axis_size(axis),) + value.shape[len(order) :])


def reduce_rows(value, axis, order):
    index = lax.axis_index(axis)
    left = sorted(order, reverse=True)
    value = value.reshape((2,) * len(left) + value.shape[1:])
    for bit in order:
        place = left.index(bit)
        mine = (index // bit) % 2
        give = lax.dynamic_index_in_dim(value, 1 - mine, place, keepdims=False)
        keep = lax.dynamic_index_in_dim(value, mine, place, keepdims=False)
        value = keep.astype(F32) + swap(give.astype(BF16), axis, bit).astype(F32)
        left.remove(bit)
    return value.astype(BF16)


def orders(axis):
    bits = bits_of(axis)
    return bits, bits[1:] + bits[:1]


def local(frames, query, keys, values, norm_gain, conv_gain, w_glu, taps, w_out, cotangent):
    groups = lax.axis_size("tm")
    copies = lax.axis_size("dp")
    mine = lax.axis_index("tm")
    rows, width = frames.shape[1:]
    length = rows * groups
    block = width // groups
    kernel = taps.shape[0]
    half = kernel // 2

    def own(arr):
        return lax.dynamic_slice_in_dim(arr, mine * block, block, arr.ndim - 1)

    norm_own, conv_own, taps_own = own(norm_gain), own(conv_gain), own(taps)

    q, k, v, res = to_channels(jnp.concatenate([query, keys, values, frames]))
    w_glu, q = lax.optimization_barrier((w_glu, q))

    columns = w_glu.reshape(block, 2, groups, block)
    tm_bits = bits_of("tm")
    offsets = [0]
    for bit in reversed(tm_bits):
        offsets = offsets + [o ^ bit for o in offsets]
    pieces = []
    for offset in offsets:
        piece = lax.dynamic_index_in_dim(columns, mine ^ offset, 2, keepdims=False)
        piece = piece.reshape(block, 2 * block)
        pieces.append(piece if offset == 0 else swap(piece, "tm", offset))
    w_own = jnp.concatenate(pieces)

    attention = attend(q, k, v, width // HEADS)
    mixed = res.astype(F32) + attention.astype(F32)
    mean, inv_u = moments(mixed)
    u_own = ((mixed - mean) * inv_u * norm_own).astype(BF16)

    parts = [u_own]
    for bit in reversed(tm_bits):
        parts = parts + [swap(part, "tm", bit) for part in parts]
    u_all = jnp.concatenate(parts, axis=1)
    cot, u_all = lax.optimization_barrier((cotangent[0], u_all))
    cot_all = gather_rows(cot, "tm", tm_bits[::-1]).reshape(length, width)

    p_own = jnp.dot(u_all, w_own, preferred_element_type=F32)
    first = p_own[:, :block]
    sig = jax.nn.sigmoid(p_own[:, block:])
    y_rows = (first * sig).astype(BF16)
    padded = jnp.pad(y_rows, ((half, half), (0, 0)))
    z_rows = jnp.zeros((length, block), F32)
    for t in range(kernel):
        z_rows = z_rows + taps_own[t] * padded[t : t + length].astype(F32)
    mean_z, inv = moments(z_rows)
    zhat = (z_rows - mean_z) * inv
    n_rows = zhat * conv_own
    sgate = jax.nn.sigmoid(n_rows)
    s_rows = (n_rows * sgate).astype(BF16)

    d_s = lax.dot_general(cot_all, w_out, (((1,), (1,)), ((), ())), preferred_element_type=F32)
    d_n = d_s * sgate * (1.0 + n_rows * (1.0 - sgate))
    e_rows = d_n * conv_own
    mean_e, mean_ez = row_means(e_rows, e_rows * zhat)
    d_z = ((e_rows - mean_e - zhat * mean_ez) * inv).astype(BF16)

    dz_pad = jnp.pad(d_z, ((half, half), (0, 0)))
    d_y = jnp.zeros((length, block), F32)
    for t in range(kernel):
        d_y = d_y + taps_own[t] * dz_pad[2 * half - t : 2 * half - t + length].astype(F32)
    d_p = jnp.concatenate([d_y * sig, d_y * first * sig * (1.0 - sig)], axis=1).astype(BF16)

    dz_float = d_z.astype(F32)
    taps_sum = jnp.stack(
        [jnp.sum(dz_float * padded[t : t + length].astype(F32), axis=0) for t in range(kernel)]
    )
    dp_bits = bits_of("dp")
    for bit in dp_bits:
        taps_sum = taps_sum + swap(taps_sum, "dp", bit)

    contract = (((0,), (0,)), ((), ()))
    share = block // copies
    near, far = orders("dp")

    def summed(value, columns):
        middle = columns // 2
        return (
            reduce_rows(value[..., :middle], "dp", near),
            reduce_rows(value[..., middle:], "dp", far),
        )

    def spread_out(pair):
        return [
            gather_rows(pair[0], "dp", near[::-1]),
            gather_rows(pair[1], "dp", far[::-1]),
        ]

    out_term = lax.dot_general(s_rows, cot_all, contract, preferred_element_type=F32)
    out_pair = summed(out_term.reshape(copies, share, width), width)
    out_grad = jnp.concatenate(
        [h.reshape(block, width // 2) for h in spread_out(out_pair)], axis=1
    ).astype(F32)

    glu_term = lax.dot_general(u_all, d_p, contract, preferred_element_type=F32)
    glu_term = glu_term.reshape(groups, copies, share, 2 * block).transpose(1, 0, 2, 3)
    halves = []
    for part in summed(glu_term, 2 * block):
        place = {offset: i for i, offset in enumerate(offsets)}
        lookup = jnp.array([place[o] for o in range(groups)], jnp.int32)
        ordered = jnp.stack(
            [
                lax.dynamic_index_in_dim(part, lookup[mine ^ g], 0, keepdims=False)
                for g in range(groups)
            ]
        )
        moved = lax.all_to_all(ordered, "tm", split_axis=0, concat_axis=0, tiled=True)
        halves.append(moved.transpose(1, 0, 2).reshape(share, width))
    glu_grad = jnp.concatenate(
        [h.reshape(block, width) for h in spread_out(halves)], axis=1
    ).astype(F32)
    return (glu_grad, taps_sum, out_grad)


def solution(mesh):
    return jax.shard_map(
        local,
        mesh=mesh,
        in_specs=(
            P("dp", "tm", None),
            P("dp", "tm", None),
            P("dp", "tm", None),
            P("dp", "tm", None),
            P(),
            P(),
            P("tm", None),
            P(),
            P("tm", None),
            P("dp", "tm", None),
        ),
        out_specs=(P("tm", None), P(None, "tm"), P("tm", None)),
        check_vma=False,
    )
```

```python
import jax
import jax.numpy as jnp
from jax import lax
from jax.experimental import pallas as pl
from jax.experimental.pallas import tpu as pltpu
from jax.sharding import PartitionSpec as P

HEADS = 16
LANES = 128
F32 = jnp.float32
BF16 = jnp.bfloat16


def bits_of(axis):
    size = lax.axis_size(axis)
    return [1 << i for i in range(size.bit_length() - 1)]


def swap(value, axis, offset):
    size = lax.axis_size(axis)
    return lax.ppermute(value, axis, [(i, i ^ offset) for i in range(size)])


def tile_width(block):
    return LANES if block % LANES == 0 else block


def as_row(column):
    return jnp.broadcast_to(column, (column.shape[0], LANES)).T[:1]


def as_column(row):
    return jnp.broadcast_to(row, (LANES, row.shape[1])).T[:, :1]


def call(body, outs, args, scratch=(), scalars=()):
    space = pl.BlockSpec(memory_space=pltpu.MemorySpace.VMEM)
    scalar = pl.BlockSpec(memory_space=pltpu.MemorySpace.SMEM)
    return pl.pallas_call(
        body,
        out_shape=[jax.ShapeDtypeStruct(shape, dtype) for shape, dtype in outs],
        in_specs=[scalar] * len(scalars) + [space] * len(args),
        out_specs=[space] * len(outs),
        scratch_shapes=list(scratch),
        compiler_params=pltpu.CompilerParams(vmem_limit_bytes=56 * 1024 * 1024),
    )(*scalars, *args)


def attend(mine, blocks, head_dim):
    groups = len(blocks)
    rows, width = blocks[0].shape[1:]
    length = groups * rows
    scale = head_dim ** (-0.5)

    def body(index, *refs):
        parts, mixed, stat = refs[:groups], refs[groups], refs[groups + 1]
        outs = [[] for _ in parts]
        for low in range(0, width, head_dim):
            cols = slice(low, low + head_dim)
            k = jnp.concatenate([part[1, :, cols] for part in parts])
            v = jnp.concatenate([part[2, :, cols] for part in parts])
            for m, part in enumerate(parts):
                scores = lax.dot_general(
                    part[0, :, cols], k, (((1,), (1,)), ((), ())), preferred_element_type=F32
                )
                scores = scores * scale
                expo = jnp.exp(scores - jnp.max(scores, axis=1, keepdims=True))
                total = jnp.sum(expo, axis=1, keepdims=True)
                summed = jnp.dot(expo.astype(BF16), v, preferred_element_type=F32)
                outs[m].append((summed / total).astype(BF16))
        for m, part in enumerate(parts):
            start = pl.multiple_of((index[0] ^ m) * rows, rows)
            value = part[3].astype(F32) + jnp.concatenate(outs[m], axis=1).astype(F32)
            mean = jnp.mean(value, axis=1, keepdims=True)
            centred = value - mean
            spread = jnp.sum(centred * centred, axis=1, keepdims=True)
            mixed[pl.ds(start, rows), :] = value
            stat[:, pl.ds(start, rows)] = jnp.concatenate([as_row(mean), as_row(spread)])

    return call(
        body, [((length, width), F32), ((2, length), F32)], blocks, scalars=[mine.reshape(1)]
    )


def normalize(value, stat, gain):
    length, width = value.shape

    def body(value_ref, stat_ref, gain_ref, out):
        for low in range(0, length, LANES):
            rows = slice(low, low + LANES)
            mean, inv = as_column(stat_ref[:1, rows]), as_column(stat_ref[1:, rows])
            out[rows] = ((value_ref[rows] - mean) * inv * gain_ref[...]).astype(BF16)

    return call(body, [((length, width), BF16)], [value, stat, gain])[0]


def fill(padded, half, length, width, read):
    tile = tile_width(width)
    for i in range(width // tile):
        padded[i, :half] = jnp.zeros((half, tile), F32)
        padded[i, half + length :] = jnp.zeros((half, tile), F32)
        for low in range(0, length, LANES):
            padded[i, half + low : half + low + LANES] = read(low, i * tile, tile)


def convolve(padded, taps, length, width, places, write, chunk=64):
    tile = tile_width(width)
    for i in range(width // tile):
        cols = slice(i * tile, (i + 1) * tile)

        def step(j, carry, i=i, cols=cols):
            start = pl.multiple_of(j * chunk, chunk)
            total = jnp.zeros((chunk, tile), F32)
            for t, place in enumerate(places):
                total = total + taps[t : t + 1, cols] * padded[i, pl.ds(start + place, chunk)]
            write(start, chunk, cols, total)
            return carry

        lax.fori_loop(0, length // chunk, step, 0)


def gate(u_parts, w_parts, taps):
    length, block = u_parts[0].shape
    count = len(u_parts)
    kernel = taps.shape[0]
    half = kernel // 2
    tile = tile_width(block)

    def body(*refs):
        us, ws, taps_ref = refs[:count], refs[count : 2 * count], refs[2 * count]
        p_ref, y_ref, z_ref, stat, padded = refs[2 * count + 1 :]
        for low in range(0, length, LANES):
            rows = slice(low, low + LANES)
            p = jnp.dot(us[0][rows], ws[0][...], preferred_element_type=F32)
            for u, w in zip(us[1:], ws[1:]):
                p = p + jnp.dot(u[rows], w[...], preferred_element_type=F32)
            p_ref[rows] = p
            y_ref[rows] = (p[:, :block] * jax.nn.sigmoid(p[:, block:])).astype(BF16)
        fill(
            padded,
            half,
            length,
            block,
            lambda low, col, size: y_ref[low : low + LANES, col : col + size].astype(F32),
        )

        def write(start, chunk, cols, total):
            z_ref[pl.ds(start, chunk), cols] = total

        convolve(padded, taps_ref, length, block, range(kernel), write)
        for low in range(0, length, LANES):
            rows = slice(low, low + LANES)
            value = z_ref[rows]
            mean = jnp.mean(value, axis=1, keepdims=True)
            centred = value - mean
            spread = jnp.sum(centred * centred, axis=1, keepdims=True)
            stat[:, rows] = jnp.concatenate([as_row(mean), as_row(spread)])

    return call(
        body,
        [
            ((length, 2 * block), F32),
            ((length, block), BF16),
            ((length, block), F32),
            ((2, length), F32),
        ],
        [*u_parts, *w_parts, taps],
        [pltpu.VMEM((block // tile, length + 2 * half, tile), F32)],
    )


def swish(z, stat, gain, d_s):
    length, block = z.shape

    def body(z_ref, stat_ref, gain_ref, ds_ref, s_ref, zhat_ref, e_ref, sums):
        for low in range(0, length, LANES):
            rows = slice(low, low + LANES)
            mean, inv = as_column(stat_ref[:1, rows]), as_column(stat_ref[1:, rows])
            zhat = (z_ref[rows] - mean) * inv
            n = zhat * gain_ref[...]
            sgate = jax.nn.sigmoid(n)
            s_ref[rows] = (n * sgate).astype(BF16)
            e = ds_ref[rows] * sgate * (1.0 + n * (1.0 - sgate)) * gain_ref[...]
            zhat_ref[rows] = zhat
            e_ref[rows] = e
            both = [jnp.sum(e, axis=1, keepdims=True), jnp.sum(e * zhat, axis=1, keepdims=True)]
            sums[:, rows] = jnp.concatenate([as_row(both[0]), as_row(both[1])])

    return call(
        body,
        [
            ((length, block), BF16),
            ((length, block), F32),
            ((length, block), F32),
            ((2, length), F32),
        ],
        [z, stat, gain, d_s],
    )


def ungate(e, zhat, stat, means, p, y, taps):
    length, block = e.shape
    kernel = taps.shape[0]
    half = kernel // 2
    tile = tile_width(block)
    group = 8

    def body(e_ref, zhat_ref, stat_ref, means_ref, p_ref, y_ref, taps_ref, dp_ref, tg_ref, *pads):
        dz_pad, y_pad, dz_all = pads
        for low in range(0, length, LANES):
            rows = slice(low, low + LANES)
            inv = as_column(stat_ref[1:, rows])
            mean, mean_z = as_column(means_ref[:1, rows]), as_column(means_ref[1:, rows])
            d_z = (e_ref[rows] - mean - zhat_ref[rows] * mean_z) * inv
            dz_all[rows] = d_z.astype(BF16).astype(F32)
        fill(
            dz_pad,
            half,
            length,
            block,
            lambda low, col, size: dz_all[low : low + LANES, col : col + size],
        )
        fill(
            y_pad,
            half,
            length,
            block,
            lambda low, col, size: y_ref[low : low + LANES, col : col + size].astype(F32),
        )

        def write(start, chunk, cols, total):
            rows = pl.ds(start, chunk)
            first = p_ref[rows, cols]
            sig = jax.nn.sigmoid(p_ref[rows, slice(block + cols.start, block + cols.stop)])
            dp_ref[rows, cols] = (total * sig).astype(BF16)
            dp_ref[rows, slice(block + cols.start, block + cols.stop)] = (
                total * first * sig * (1.0 - sig)
            ).astype(BF16)

        convolve(
            dz_pad, taps_ref, length, block, [2 * half - t for t in range(kernel)], write
        )
        for i in range(block // tile):

            def step(j, sums, i=i):
                start = pl.multiple_of(j * group, group)
                d_z = dz_pad[i, pl.ds(start + half, group)]
                return tuple(
                    total + d_z * y_pad[i, pl.ds(start + t, group)]
                    for t, total in enumerate(sums)
                )

            zero = jnp.zeros((group, tile), F32)
            sums = lax.fori_loop(0, length // group, step, (zero,) * kernel)
            tg_ref[:, i * tile : (i + 1) * tile] = jnp.concatenate(
                [jnp.sum(total, axis=0, keepdims=True) for total in sums]
            )

    pad = pltpu.VMEM((block // tile, length + 2 * half, tile), F32)
    return call(
        body,
        [((length, 2 * block), BF16), ((kernel, block), F32)],
        [e, zhat, stat, means, p, y, taps],
        [pad, pad, pltpu.VMEM((length, block), F32)],
    )


def merge_moments(stat, count):
    for bit in bits_of("tm"):
        other = swap(stat, "tm", bit)
        gap = stat[:1] - other[:1]
        stat = jnp.concatenate(
            [
                0.5 * (stat[:1] + other[:1]),
                stat[1:] + other[1:] + gap * gap * (0.5 * count),
            ]
        )
        count = 2 * count
    return jnp.concatenate([stat[:1], lax.rsqrt(stat[1:] / count + 1e-05)])


def merge_means(sums, count):
    for bit in bits_of("tm"):
        sums = sums + swap(sums, "tm", bit)
    return sums / count


def gather_rows(value, axis, order):
    index = lax.axis_index(axis)
    value = value[(None,) * len(order)]
    for bit in order:
        other = swap(value, axis, bit)
        upper = (index // bit) % 2 == 1
        place = len(order) - bit.bit_length()
        value = jnp.concatenate(
            [jnp.where(upper, other, value), jnp.where(upper, value, other)], axis=place
        )
    return value.reshape((lax.axis_size(axis),) + value.shape[len(order) :])


def reduce_rows(value, axis, order):
    index = lax.axis_index(axis)
    left = sorted(order, reverse=True)
    value = value.reshape((2,) * len(left) + value.shape[1:])
    for bit in order:
        place = left.index(bit)
        mine = (index // bit) % 2
        give = lax.dynamic_index_in_dim(value, 1 - mine, place, keepdims=False)
        keep = lax.dynamic_index_in_dim(value, mine, place, keepdims=False)
        value = keep.astype(F32) + swap(give.astype(BF16), axis, bit).astype(F32)
        left.remove(bit)
    return value.astype(BF16)


def orders(axis):
    bits = bits_of(axis)
    return bits, bits[1:] + bits[:1]


def local(frames, query, keys, values, norm_gain, conv_gain, w_glu, taps, w_out, cotangent):
    groups = lax.axis_size("tm")
    copies = lax.axis_size("dp")
    mine = lax.axis_index("tm")
    rows, width = frames.shape[1:]
    length = rows * groups
    block = width // groups
    share = block // copies
    tm_bits = bits_of("tm")
    offsets = [0]
    for bit in reversed(tm_bits):
        offsets = offsets + [o ^ bit for o in offsets]
    near, far = orders("dp")

    def columns(arr, owner, low=0):
        return lax.dynamic_slice_in_dim(arr, owner * block + low, block, arr.ndim - 1)

    norm_own = columns(norm_gain[None], mine)
    conv_own = columns(conv_gain[None], mine)
    taps_own = columns(taps, mine)

    def glu_columns(arr, owner):
        return jnp.concatenate([columns(arr, owner), columns(arr, owner, width)], axis=1)

    place = lax.axis_index("dp") * share
    w_share = lax.dynamic_slice_in_dim(w_glu, place, share, 0)
    w_parts = {0: glu_columns(w_glu, mine), 1: swap(glu_columns(w_glu, mine ^ 1), "tm", 1)}
    distant = [o for o in offsets if o > 1]
    if distant:
        fetched = jnp.stack([swap(glu_columns(w_share, mine ^ o), "tm", o) for o in distant])

    stacked = jnp.concatenate([query, keys, values, frames])
    blocks = []
    for m in range(groups):
        piece = columns(stacked, mine ^ m)
        blocks.append(piece if m == 0 else swap(piece, "tm", m))

    if distant:
        spread = jnp.concatenate(
            [
                gather_rows(fetched[..., :block], "dp", near[::-1]),
                gather_rows(fetched[..., block:], "dp", far[::-1]),
            ],
            axis=-1,
        )
        for i, offset in enumerate(distant):
            w_parts[offset] = spread[:, i].reshape(block, 2 * block)

    mixed, stat_u = attend(mine, blocks, width // HEADS)
    stat_u = merge_moments(stat_u, block)
    u_own = normalize(mixed, stat_u, norm_own)

    u_parts = [u_own]
    for bit in reversed(tm_bits):
        u_parts = u_parts + [swap(part, "tm", bit) for part in u_parts]
    cot, u_parts[-1] = lax.optimization_barrier((cotangent[0], u_parts[-1]))
    cot_all = gather_rows(cot, "tm", tm_bits[::-1]).reshape(length, width)
    d_s = lax.dot_general(cot_all, w_out, (((1,), (1,)), ((), ())), preferred_element_type=F32)

    p_own, y_rows, z_rows, stat_z = gate(u_parts, [w_parts[o] for o in offsets], taps_own)
    stat_z = merge_moments(stat_z, block)
    s_rows, zhat, e_rows, sums = swish(z_rows, stat_z, conv_own, d_s)
    means = merge_means(sums, width)
    d_p, taps_sum = ungate(e_rows, zhat, stat_z, means, p_own, y_rows, taps_own)
    u_all = jnp.concatenate(u_parts, axis=1)
    for bit in near:
        taps_sum = taps_sum + swap(taps_sum, "dp", bit)

    contract = (((0,), (0,)), ((), ()))

    def summed(value, count):
        middle = count // 2
        return (
            reduce_rows(value[..., :middle], "dp", near),
            reduce_rows(value[..., middle:], "dp", far),
        )

    def spread_out(pair):
        return [
            gather_rows(pair[0], "dp", near[::-1]),
            gather_rows(pair[1], "dp", far[::-1]),
        ]

    out_term = lax.dot_general(s_rows, cot_all, contract, preferred_element_type=F32)
    out_pair = summed(out_term.reshape(copies, share, width), width)
    out_grad = jnp.concatenate(
        [h.reshape(block, width // 2) for h in spread_out(out_pair)], axis=1
    ).astype(F32)

    glu_term = lax.dot_general(u_all, d_p, contract, preferred_element_type=F32)
    glu_term = glu_term.reshape(groups, copies, share, 2 * block).transpose(1, 0, 2, 3)
    halves = []
    for part in summed(glu_term, 2 * block):
        place = {offset: i for i, offset in enumerate(offsets)}
        lookup = jnp.array([place[o] for o in range(groups)], jnp.int32)
        ordered = jnp.stack(
            [
                lax.dynamic_index_in_dim(part, lookup[mine ^ g], 0, keepdims=False)
                for g in range(groups)
            ]
        )
        moved = lax.all_to_all(ordered, "tm", split_axis=0, concat_axis=0, tiled=True)
        halves.append(moved.transpose(1, 0, 2).reshape(share, width))
    glu_grad = jnp.concatenate(
        [h.reshape(block, width) for h in spread_out(halves)], axis=1
    ).astype(F32)
    return (glu_grad, taps_sum, out_grad)


def solution(mesh):
    return jax.shard_map(
        local,
        mesh=mesh,
        in_specs=(
            P("dp", "tm", None),
            P("dp", "tm", None),
            P("dp", "tm", None),
            P("dp", "tm", None),
            P(),
            P(),
            P("tm", None),
            P(),
            P("tm", None),
            P("dp", "tm", None),
        ),
        out_specs=(P("tm", None), P(None, "tm"), P("tm", None)),
        check_vma=False,
    )
```

```python
import jax
import jax.numpy as jnp
from jax import lax
from jax.experimental import pallas as pl
from jax.experimental.pallas import tpu as pltpu
from jax.sharding import PartitionSpec as P

HEADS = 16
LANES = 128
F32 = jnp.float32
BF16 = jnp.bfloat16


def bits_of(axis):
    size = lax.axis_size(axis)
    return [1 << i for i in range(size.bit_length() - 1)]


def swap(value, axis, offset):
    size = lax.axis_size(axis)
    return lax.ppermute(value, axis, [(i, i ^ offset) for i in range(size)])


def tile_width(block):
    return LANES if block % LANES == 0 else block


def as_row(column):
    return jnp.broadcast_to(column, (column.shape[0], LANES)).T[:1]


def as_column(row):
    return jnp.broadcast_to(row, (LANES, row.shape[1])).T[:, :1]


def call(body, outs, args, scratch=(), scalars=()):
    space = pl.BlockSpec(memory_space=pltpu.MemorySpace.VMEM)
    scalar = pl.BlockSpec(memory_space=pltpu.MemorySpace.SMEM)
    return pl.pallas_call(
        body,
        out_shape=[jax.ShapeDtypeStruct(shape, dtype) for shape, dtype in outs],
        in_specs=[scalar] * len(scalars) + [space] * len(args),
        out_specs=[space] * len(outs),
        scratch_shapes=list(scratch),
        compiler_params=pltpu.CompilerParams(vmem_limit_bytes=56 * 1024 * 1024),
    )(*scalars, *args)


def attend(mine, blocks, residual, head_dim):
    groups = len(blocks)
    rows, width = blocks[0].shape[1:]
    length = groups * rows
    scale = head_dim ** (-0.5)

    def body(index, *refs):
        parts, rest, (mixed, stat) = refs[:groups], refs[groups : 2 * groups], refs[2 * groups :]
        outs = [[] for _ in parts]
        for low in range(0, width, head_dim):
            cols = slice(low, low + head_dim)
            k = jnp.concatenate([part[1, :, cols] for part in parts])
            v = jnp.concatenate([part[2, :, cols] for part in parts])
            for m, part in enumerate(parts):
                scores = lax.dot_general(
                    part[0, :, cols], k, (((1,), (1,)), ((), ())), preferred_element_type=F32
                )
                scores = scores * scale
                expo = jnp.exp(scores - jnp.max(scores, axis=1, keepdims=True))
                total = jnp.sum(expo, axis=1, keepdims=True)
                summed = jnp.dot(expo.astype(BF16), v, preferred_element_type=F32)
                outs[m].append((summed / total).astype(BF16))
        for m, part in enumerate(rest):
            start = pl.multiple_of((index[0] ^ m) * rows, rows)
            value = part[0].astype(F32) + jnp.concatenate(outs[m], axis=1).astype(F32)
            mean = jnp.mean(value, axis=1, keepdims=True)
            centred = value - mean
            spread = jnp.sum(centred * centred, axis=1, keepdims=True)
            mixed[pl.ds(start, rows), :] = value
            stat[:, pl.ds(start, rows)] = jnp.concatenate([as_row(mean), as_row(spread)])

    return call(
        body, [((length, width), F32), ((2, length), F32)],
        [*blocks, *residual],
        scalars=[mine.reshape(1)],
    )


def normalize(value, stat, gain):
    length, width = value.shape

    def body(value_ref, stat_ref, gain_ref, out):
        for low in range(0, length, LANES):
            rows = slice(low, low + LANES)
            mean, inv = as_column(stat_ref[:1, rows]), as_column(stat_ref[1:, rows])
            out[rows] = ((value_ref[rows] - mean) * inv * gain_ref[...]).astype(BF16)

    return call(body, [((length, width), BF16)], [value, stat, gain])[0]


def fill(padded, half, length, width, read):
    tile = tile_width(width)
    for i in range(width // tile):
        padded[i, :half] = jnp.zeros((half, tile), F32)
        padded[i, half + length :] = jnp.zeros((half, tile), F32)
        for low in range(0, length, LANES):
            padded[i, half + low : half + low + LANES] = read(low, i * tile, tile)


def convolve(padded, taps, length, width, places, write, chunk=64):
    tile = tile_width(width)
    for i in range(width // tile):
        cols = slice(i * tile, (i + 1) * tile)

        def step(j, carry, i=i, cols=cols):
            start = pl.multiple_of(j * chunk, chunk)
            total = jnp.zeros((chunk, tile), F32)
            for t, place in enumerate(places):
                total = total + taps[t : t + 1, cols] * padded[i, pl.ds(start + place, chunk)]
            write(start, chunk, cols, total)
            return carry

        lax.fori_loop(0, length // chunk, step, 0)


def gate(u_parts, w_parts, taps):
    length, block = u_parts[0].shape
    count = len(u_parts)
    kernel = taps.shape[0]
    half = kernel // 2
    tile = tile_width(block)

    def body(*refs):
        us, ws, taps_ref = refs[:count], refs[count : 2 * count], refs[2 * count]
        p_ref, y_ref, z_ref, stat, padded = refs[2 * count + 1 :]
        for low in range(0, length, LANES):
            rows = slice(low, low + LANES)
            p = jnp.dot(us[0][rows], ws[0][...], preferred_element_type=F32)
            for u, w in zip(us[1:], ws[1:]):
                p = p + jnp.dot(u[rows], w[...], preferred_element_type=F32)
            p_ref[rows] = p
            y_ref[rows] = (p[:, :block] * jax.nn.sigmoid(p[:, block:])).astype(BF16)
        fill(
            padded,
            half,
            length,
            block,
            lambda low, col, size: y_ref[low : low + LANES, col : col + size].astype(F32),
        )

        def write(start, chunk, cols, total):
            z_ref[pl.ds(start, chunk), cols] = total

        convolve(padded, taps_ref, length, block, range(kernel), write)
        for low in range(0, length, LANES):
            rows = slice(low, low + LANES)
            value = z_ref[rows]
            mean = jnp.mean(value, axis=1, keepdims=True)
            centred = value - mean
            spread = jnp.sum(centred * centred, axis=1, keepdims=True)
            stat[:, rows] = jnp.concatenate([as_row(mean), as_row(spread)])

    return call(
        body,
        [
            ((length, 2 * block), F32),
            ((length, block), BF16),
            ((length, block), F32),
            ((2, length), F32),
        ],
        [*u_parts, *w_parts, taps],
        [pltpu.VMEM((block // tile, length + 2 * half, tile), F32)],
    )


def swish(z, stat, gain, d_s):
    length, block = z.shape

    def body(z_ref, stat_ref, gain_ref, ds_ref, s_ref, zhat_ref, e_ref, sums):
        for low in range(0, length, LANES):
            rows = slice(low, low + LANES)
            mean, inv = as_column(stat_ref[:1, rows]), as_column(stat_ref[1:, rows])
            zhat = (z_ref[rows] - mean) * inv
            n = zhat * gain_ref[...]
            sgate = jax.nn.sigmoid(n)
            s_ref[rows] = (n * sgate).astype(BF16)
            e = ds_ref[rows] * sgate * (1.0 + n * (1.0 - sgate)) * gain_ref[...]
            zhat_ref[rows] = zhat
            e_ref[rows] = e
            both = [jnp.sum(e, axis=1, keepdims=True), jnp.sum(e * zhat, axis=1, keepdims=True)]
            sums[:, rows] = jnp.concatenate([as_row(both[0]), as_row(both[1])])

    return call(
        body,
        [
            ((length, block), BF16),
            ((length, block), F32),
            ((length, block), F32),
            ((2, length), F32),
        ],
        [z, stat, gain, d_s],
    )


def ungate(e, zhat, stat, means, p, taps):
    length, block = e.shape
    kernel = taps.shape[0]
    half = kernel // 2
    tile = tile_width(block)

    def body(e_ref, zhat_ref, stat_ref, means_ref, p_ref, taps_ref, dp_ref, dz_ref, padded):
        for low in range(0, length, LANES):
            rows = slice(low, low + LANES)
            inv = as_column(stat_ref[1:, rows])
            mean, mean_z = as_column(means_ref[:1, rows]), as_column(means_ref[1:, rows])
            d_z = (e_ref[rows] - mean - zhat_ref[rows] * mean_z) * inv
            dz_ref[rows] = d_z.astype(BF16)
        fill(
            padded,
            half,
            length,
            block,
            lambda low, col, size: dz_ref[low : low + LANES, col : col + size].astype(F32),
        )

        def write(start, chunk, cols, total):
            rows = pl.ds(start, chunk)
            first = p_ref[rows, cols]
            sig = jax.nn.sigmoid(p_ref[rows, slice(block + cols.start, block + cols.stop)])
            dp_ref[rows, cols] = (total * sig).astype(BF16)
            dp_ref[rows, slice(block + cols.start, block + cols.stop)] = (
                total * first * sig * (1.0 - sig)
            ).astype(BF16)

        convolve(
            padded, taps_ref, length, block, [2 * half - t for t in range(kernel)], write
        )

    return call(
        body,
        [((length, 2 * block), BF16), ((length, block), BF16)],
        [e, zhat, stat, means, p, taps],
        [pltpu.VMEM((block // tile, length + 2 * half, tile), F32)],
    )


def taps_gradient(d_z, y, kernel):
    length, block = y.shape
    half = kernel // 2
    tile = tile_width(block)
    group = 8

    def body(dz_ref, y_ref, out, dz_all, y_pad):
        for ref, padded in ((dz_ref, dz_all), (y_ref, y_pad)):
            fill(
                padded,
                half,
                length,
                block,
                lambda low, col, size, ref=ref: ref[low : low + LANES, col : col + size].astype(F32),
            )
        for i in range(block // tile):

            def step(j, sums, i=i):
                start = pl.multiple_of(j * group, group)
                value = dz_all[i, pl.ds(start + half, group)]
                return tuple(
                    total + value * y_pad[i, pl.ds(start + t, group)]
                    for t, total in enumerate(sums)
                )

            zero = jnp.zeros((group, tile), F32)
            sums = lax.fori_loop(0, length // group, step, (zero,) * kernel)
            out[:, i * tile : (i + 1) * tile] = jnp.concatenate(
                [jnp.sum(total, axis=0, keepdims=True) for total in sums]
            )

    pad = pltpu.VMEM((block // tile, length + 2 * half, tile), F32)
    return call(body, [((kernel, block), F32)], [d_z, y], [pad, pad])[0]


def merge_moments(stat, count):
    for bit in bits_of("tm"):
        other = swap(stat, "tm", bit)
        gap = stat[:1] - other[:1]
        stat = jnp.concatenate(
            [
                0.5 * (stat[:1] + other[:1]),
                stat[1:] + other[1:] + gap * gap * (0.5 * count),
            ]
        )
        count = 2 * count
    return jnp.concatenate([stat[:1], lax.rsqrt(stat[1:] / count + 1e-05)])


def merge_means(sums, count):
    for bit in bits_of("tm"):
        sums = sums + swap(sums, "tm", bit)
    return sums / count


def gather_rows(value, axis, order):
    index = lax.axis_index(axis)
    value = value[(None,) * len(order)]
    for bit in order:
        other = swap(value, axis, bit)
        upper = (index // bit) % 2 == 1
        place = len(order) - bit.bit_length()
        value = jnp.concatenate(
            [jnp.where(upper, other, value), jnp.where(upper, value, other)], axis=place
        )
    return value.reshape((lax.axis_size(axis),) + value.shape[len(order) :])


class Halving:
    def __init__(self, value, axis, order):
        self.axis, self.order = axis, list(order)
        self.left = sorted(order, reverse=True)
        self.value = value.reshape((2,) * len(order) + value.shape[1:])
        self.give = None

    def split(self):
        bit = self.order.pop(0)
        place = self.left.index(bit)
        self.left.remove(bit)
        mine = (lax.axis_index(self.axis) // bit) % 2
        self.bit = bit
        self.give = lax.dynamic_index_in_dim(self.value, 1 - mine, place, keepdims=False)
        self.give = self.give.astype(BF16)
        self.value = lax.dynamic_index_in_dim(self.value, mine, place, keepdims=False)

    def join(self):
        got = swap(self.give, self.axis, self.bit)
        self.value = self.value.astype(F32) + got.astype(F32)
        self.give = None


def together(items, *others):
    fixed = lax.optimization_barrier((tuple(item.give for item in items), others))
    for item, give in zip(items, fixed[0]):
        item.give = give
    return fixed[1]


def orders(axis):
    bits = bits_of(axis)
    return bits, bits[1:] + bits[:1]


def local(frames, query, keys, values, norm_gain, conv_gain, w_glu, taps, w_out, cotangent):
    groups = lax.axis_size("tm")
    copies = lax.axis_size("dp")
    mine = lax.axis_index("tm")
    rows, width = frames.shape[1:]
    length = rows * groups
    block = width // groups
    share = block // copies
    tm_bits = bits_of("tm")
    offsets = [0]
    for bit in reversed(tm_bits):
        offsets = offsets + [o ^ bit for o in offsets]
    near, far = orders("dp")

    def columns(arr, owner, low=0):
        return lax.dynamic_slice_in_dim(arr, owner * block + low, block, arr.ndim - 1)

    norm_own = columns(norm_gain[None], mine)
    conv_own = columns(conv_gain[None], mine)
    taps_own = columns(taps, mine)

    def glu_columns(arr, owner):
        return jnp.concatenate([columns(arr, owner), columns(arr, owner, width)], axis=1)

    distant = [o for o in offsets if o > 1]
    if distant:
        place = lax.axis_index("dp") * share
        w_share = lax.dynamic_slice_in_dim(w_glu, place, share, 0)
        fetched = jnp.stack([swap(glu_columns(w_share, mine ^ o), "tm", o) for o in distant])

    def exchange(arrays):
        blocks = []
        for m in range(groups):
            piece = jnp.concatenate([columns(arr, mine ^ m) for arr in arrays])
            blocks.append(piece if m == 0 else swap(piece, "tm", m))
        return blocks

    blocks = exchange([query, keys, values])
    if distant:
        fetched, frames = lax.optimization_barrier((fetched, frames))
    residual = exchange([frames])
    w_parts = {0: glu_columns(w_glu, mine), 1: swap(glu_columns(w_glu, mine ^ 1), "tm", 1)}

    if distant:
        spread = jnp.concatenate(
            [
                gather_rows(fetched[..., :block], "dp", near[::-1]),
                gather_rows(fetched[..., block:], "dp", far[::-1]),
            ],
            axis=-1,
        )
        for i, offset in enumerate(distant):
            w_parts[offset] = spread[:, i].reshape(block, 2 * block)

    cot, blocks[-1] = lax.optimization_barrier((cotangent[0], blocks[-1]))
    mixed, stat_u = attend(mine, blocks, residual, width // HEADS)
    stat_u = merge_moments(stat_u, block)
    u_own = normalize(mixed, stat_u, norm_own)

    u_parts = [u_own]
    for bit in reversed(tm_bits):
        u_parts = u_parts + [swap(part, "tm", bit) for part in u_parts]
    cot_all = gather_rows(cot, "tm", tm_bits[::-1]).reshape(length, width)
    d_s = lax.dot_general(cot_all, w_out, (((1,), (1,)), ((), ())), preferred_element_type=F32)

    p_own, y_rows, z_rows, stat_z = gate(u_parts, [w_parts[o] for o in offsets], taps_own)
    stat_z = merge_moments(stat_z, block)
    s_rows, zhat, e_rows, sums = swish(z_rows, stat_z, conv_own, d_s)
    contract = (((0,), (0,)), ((), ()))
    middle = width // 2
    out_term = lax.dot_general(s_rows, cot_all, contract, preferred_element_type=F32)
    out_term = out_term.reshape(copies, share, width)
    outs = [Halving(out_term[..., :middle], "dp", near), Halving(out_term[..., middle:], "dp", far)]
    steps = len(near)
    for item in outs:
        item.split()
    (sums,) = together(outs, sums)
    for item in outs:
        item.join()

    means = merge_means(sums, width)
    d_p, d_z = ungate(e_rows, zhat, stat_z, means, p_own, taps_own)
    if steps > 1:
        for item in outs:
            item.split()
        (d_p,) = together(outs, d_p)
        for item in outs:
            item.join()

    u_all = jnp.concatenate(u_parts, axis=1)
    glu_term = lax.dot_general(u_all, d_p, contract, preferred_element_type=F32)
    glu_term = glu_term.reshape(groups, copies, share, 2 * block).transpose(1, 0, 2, 3)
    glus = [Halving(glu_term[..., :block], "dp", near), Halving(glu_term[..., block:], "dp", far)]
    for item in glus:
        item.split()
    d_z, y_rows = together(glus, d_z, y_rows)
    taps_sum = taps_gradient(d_z, y_rows, taps.shape[0])
    for item in glus:
        item.join()
    for i in range(1, steps):
        for item in glus:
            item.split()
        (taps_sum,) = together(glus[:1], taps_sum)
        if i + 1 < steps:
            for item in outs:
                item.split()
            together(glus[:1] + outs)
            for item in outs:
                item.join()
        taps_sum = taps_sum + swap(taps_sum, "dp", near[i - 1])
        for item in glus:
            item.join()

    index = {offset: i for i, offset in enumerate(offsets)}
    lookup = jnp.array([index[o] for o in range(groups)], jnp.int32)
    pieces = []
    for item, out in zip(glus, outs):
        part = item.value.astype(BF16)
        got = [part[0]] + [swap(part[i], "tm", o) for i, o in enumerate(offsets) if i > 0]
        got = jnp.stack(got)
        ordered = [
            lax.dynamic_index_in_dim(got, lookup[mine ^ g], 0, keepdims=False)
            for g in range(groups)
        ]
        pieces.append(jnp.concatenate(ordered + [out.value.astype(BF16)], axis=1))
    (taps_sum, pieces[0]) = lax.optimization_barrier((taps_sum, pieces[0]))
    taps_sum = taps_sum + swap(taps_sum, "dp", near[-1])

    spread = [
        gather_rows(pieces[0], "dp", near[::-1]).reshape(block, width + middle),
        gather_rows(pieces[1], "dp", far[::-1]).reshape(block, width + middle),
    ]
    glu_grad = jnp.concatenate([half[:, :width] for half in spread], axis=1).astype(F32)
    out_grad = jnp.concatenate([half[:, width:] for half in spread], axis=1).astype(F32)
    return (glu_grad, taps_sum, out_grad)


def solution(mesh):
    return jax.shard_map(
        local,
        mesh=mesh,
        in_specs=(
            P("dp", "tm", None),
            P("dp", "tm", None),
            P("dp", "tm", None),
            P("dp", "tm", None),
            P(),
            P(),
            P("tm", None),
            P(),
            P("tm", None),
            P("dp", "tm", None),
        ),
        out_specs=(P("tm", None), P(None, "tm"), P("tm", None)),
        check_vma=False,
    )
```

```python
import jax
import jax.numpy as jnp
from jax import lax
from jax.experimental import pallas as pl
from jax.experimental.pallas import tpu as pltpu
from jax.sharding import PartitionSpec as P

HEADS = 16
LANES = 128
F32 = jnp.float32
BF16 = jnp.bfloat16


def bits_of(axis):
    size = lax.axis_size(axis)
    return [1 << i for i in range(size.bit_length() - 1)]


def swap(value, axis, offset):
    size = lax.axis_size(axis)
    return lax.ppermute(value, axis, [(i, i ^ offset) for i in range(size)])


def index_of(axis):
    return lax.axis_index(axis).astype(jnp.uint32)


def tile_width(block):
    return LANES if block % LANES == 0 else block


def as_row(column):
    return jnp.broadcast_to(column, (column.shape[0], LANES)).T[:1]


def as_column(row):
    return jnp.broadcast_to(row, (LANES, row.shape[1])).T[:, :1]


def call(body, outs, args, scratch=(), scalars=()):
    space = pl.BlockSpec(memory_space=pltpu.MemorySpace.VMEM)
    scalar = pl.BlockSpec(memory_space=pltpu.MemorySpace.SMEM)
    return pl.pallas_call(
        body,
        out_shape=[jax.ShapeDtypeStruct(shape, dtype) for shape, dtype in outs],
        in_specs=[scalar] * len(scalars) + [space] * len(args),
        out_specs=[space] * len(outs),
        scratch_shapes=list(scratch),
        compiler_params=pltpu.CompilerParams(vmem_limit_bytes=56 * 1024 * 1024),
    )(*scalars, *args)


def attend(mine, blocks, residual, head_dim):
    groups = len(blocks)
    rows, width = blocks[0].shape[1:]
    length = groups * rows
    scale = head_dim ** (-0.5)

    def body(index, *refs):
        parts, rest, (mixed, stat) = refs[:groups], refs[groups : 2 * groups], refs[2 * groups :]
        outs = [[] for _ in parts]
        for low in range(0, width, head_dim):
            cols = slice(low, low + head_dim)
            k = jnp.concatenate([part[1, :, cols] for part in parts])
            v = jnp.concatenate([part[2, :, cols] for part in parts])
            for m, part in enumerate(parts):
                scores = lax.dot_general(
                    part[0, :, cols], k, (((1,), (1,)), ((), ())), preferred_element_type=F32
                )
                scores = scores * scale
                expo = jnp.exp(scores - jnp.max(scores, axis=1, keepdims=True))
                total = jnp.sum(expo, axis=1, keepdims=True)
                summed = jnp.dot(expo.astype(BF16), v, preferred_element_type=F32)
                outs[m].append((summed / total).astype(BF16))
        for m, part in enumerate(rest):
            start = pl.multiple_of((index[0] ^ m) * rows, rows)
            value = part[0].astype(F32) + jnp.concatenate(outs[m], axis=1).astype(F32)
            mean = jnp.mean(value, axis=1, keepdims=True)
            centred = value - mean
            spread = jnp.sum(centred * centred, axis=1, keepdims=True)
            mixed[pl.ds(start, rows), :] = value.astype(BF16)
            stat[:, pl.ds(start, rows)] = jnp.concatenate([as_row(mean), as_row(spread)])

    return call(
        body, [((length, width), BF16), ((2, length), F32)],
        [*blocks, *residual],
        scalars=[mine.astype(jnp.int32).reshape(1)],
    )


def fill(padded, half, length, width, read):
    tile = tile_width(width)
    for i in range(width // tile):
        padded[i, :half] = jnp.zeros((half, tile), F32)
        padded[i, half + length :] = jnp.zeros((half, tile), F32)
        for low in range(0, length, LANES):
            padded[i, half + low : half + low + LANES] = read(low, i * tile, tile)


def convolve(padded, taps, length, width, places, write, chunk=64):
    tile = tile_width(width)
    for i in range(width // tile):
        cols = slice(i * tile, (i + 1) * tile)

        def step(j, carry, i=i, cols=cols):
            start = pl.multiple_of(j * chunk, chunk)
            total = jnp.zeros((chunk, tile), F32)
            for t, place in enumerate(places):
                total = total + taps[t : t + 1, cols] * padded[i, pl.ds(start + place, chunk)]
            write(start, chunk, cols, total)
            return carry

        lax.fori_loop(0, length // chunk, step, 0)


def gate(parts, stat_in, gain, w_near, w_far, taps):
    length, block = parts[0].shape
    count = len(parts)
    kernel = taps.shape[0]
    half = kernel // 2
    tile = tile_width(block)

    close, copies = len(w_near), len(w_far)

    def body(index, *refs):
        ins, ws, far = refs[:count], list(refs[count : count + close]), refs[count + close :]
        far, refs = far[:copies], far[copies:]
        stat_ref, gain_ref, taps_ref, u_ref, p_ref, y_ref, z_ref, stat, padded = refs[:9]
        if copies:
            whole = refs[9]
            share = far[0].shape[1]
            for offset, ref in enumerate(far):
                start = pl.multiple_of((index[0] ^ offset) * share, share)
                for m in range(count - close):
                    whole[m, pl.ds(start, share), :] = ref[m]
            ws += [whole.at[m] for m in range(count - close)]
        for low in range(0, length, LANES):
            rows = slice(low, low + LANES)
            mean, inv = as_column(stat_ref[:1, rows]), as_column(stat_ref[1:, rows])
            p = jnp.zeros((LANES, 2 * block), F32)
            for m, (part, w) in enumerate(zip(ins, ws)):
                u = (part[rows].astype(F32) - mean) * inv * gain_ref[m : m + 1]
                u = u.astype(BF16)
                u_ref[rows, m * block : (m + 1) * block] = u
                p = p + jnp.dot(u, w[...], preferred_element_type=F32)
            p_ref[rows] = p
            y_ref[rows] = (p[:, :block] * jax.nn.sigmoid(p[:, block:])).astype(BF16)
        fill(
            padded,
            half,
            length,
            block,
            lambda low, col, size: y_ref[low : low + LANES, col : col + size].astype(F32),
        )

        def write(start, chunk, cols, total):
            z_ref[pl.ds(start, chunk), cols] = total

        convolve(padded, taps_ref, length, block, range(kernel), write)
        for low in range(0, length, LANES):
            rows = slice(low, low + LANES)
            value = z_ref[rows]
            mean = jnp.mean(value, axis=1, keepdims=True)
            centred = value - mean
            spread = jnp.sum(centred * centred, axis=1, keepdims=True)
            stat[:, rows] = jnp.concatenate([as_row(mean), as_row(spread)])

    return call(
        body,
        [
            ((length, count * block), BF16),
            ((length, 2 * block), F32),
            ((length, block), BF16),
            ((length, block), F32),
            ((2, length), F32),
        ],
        [*parts, *w_near, *w_far, stat_in, gain, taps],
        [pltpu.VMEM((block // tile, length + 2 * half, tile), F32)]
        + ([pltpu.VMEM((count - close, block, 2 * block), BF16)] if copies else []),
        scalars=[index_of("dp").astype(jnp.int32).reshape(1)],
    )


def swish(z, stat, gain, d_s):
    length, block = z.shape

    def body(z_ref, stat_ref, gain_ref, ds_ref, s_ref, zhat_ref, e_ref, sums):
        for low in range(0, length, LANES):
            rows = slice(low, low + LANES)
            mean, inv = as_column(stat_ref[:1, rows]), as_column(stat_ref[1:, rows])
            zhat = (z_ref[rows] - mean) * inv
            n = zhat * gain_ref[...]
            sgate = jax.nn.sigmoid(n)
            s_ref[:, rows] = (n * sgate).T.astype(BF16)
            e = ds_ref[rows] * sgate * (1.0 + n * (1.0 - sgate)) * gain_ref[...]
            zhat_ref[rows] = zhat
            e_ref[rows] = e
            both = [jnp.sum(e, axis=1, keepdims=True), jnp.sum(e * zhat, axis=1, keepdims=True)]
            sums[:, rows] = jnp.concatenate([as_row(both[0]), as_row(both[1])])

    return call(
        body,
        [
            ((block, length), BF16),
            ((length, block), F32),
            ((length, block), F32),
            ((2, length), F32),
        ],
        [z, stat, gain, d_s],
    )


def ungate(e, zhat, stat, means, p, taps):
    length, block = e.shape
    kernel = taps.shape[0]
    half = kernel // 2
    tile = tile_width(block)

    def body(e_ref, zhat_ref, stat_ref, means_ref, p_ref, taps_ref, dp_ref, dz_ref, padded):
        for low in range(0, length, LANES):
            rows = slice(low, low + LANES)
            inv = as_column(stat_ref[1:, rows])
            mean, mean_z = as_column(means_ref[:1, rows]), as_column(means_ref[1:, rows])
            d_z = (e_ref[rows] - mean - zhat_ref[rows] * mean_z) * inv
            dz_ref[rows] = d_z.astype(BF16)
        fill(
            padded,
            half,
            length,
            block,
            lambda low, col, size: dz_ref[low : low + LANES, col : col + size].astype(F32),
        )

        def write(start, chunk, cols, total):
            rows = pl.ds(start, chunk)
            first = p_ref[rows, cols]
            sig = jax.nn.sigmoid(p_ref[rows, slice(block + cols.start, block + cols.stop)])
            dp_ref[rows, cols] = (total * sig).astype(BF16)
            dp_ref[rows, slice(block + cols.start, block + cols.stop)] = (
                total * first * sig * (1.0 - sig)
            ).astype(BF16)

        convolve(
            padded, taps_ref, length, block, [2 * half - t for t in range(kernel)], write
        )

    return call(
        body,
        [((length, 2 * block), BF16), ((length, block), BF16)],
        [e, zhat, stat, means, p, taps],
        [pltpu.VMEM((block // tile, length + 2 * half, tile), F32)],
    )


def taps_gradient(d_z, y, kernel):
    length, block = y.shape
    half = kernel // 2
    tile = tile_width(block)
    group = 8

    def body(dz_ref, y_ref, out, dz_all, y_pad):
        for ref, padded in ((dz_ref, dz_all), (y_ref, y_pad)):
            fill(
                padded,
                half,
                length,
                block,
                lambda low, col, size, ref=ref: ref[low : low + LANES, col : col + size].astype(F32),
            )
        for i in range(block // tile):

            def step(j, sums, i=i):
                start = pl.multiple_of(j * group, group)
                value = dz_all[i, pl.ds(start + half, group)]
                return tuple(
                    total + value * y_pad[i, pl.ds(start + t, group)]
                    for t, total in enumerate(sums)
                )

            zero = jnp.zeros((group, tile), F32)
            sums = lax.fori_loop(0, length // group, step, (zero,) * kernel)
            out[:, i * tile : (i + 1) * tile] = jnp.concatenate(
                [jnp.sum(total, axis=0, keepdims=True) for total in sums]
            )

    pad = pltpu.VMEM((block // tile, length + 2 * half, tile), F32)
    return call(body, [((kernel, block), F32)], [d_z, y], [pad, pad])[0]


def merge_moments(stat, count):
    for bit in bits_of("tm"):
        other = swap(stat, "tm", bit)
        gap = stat[:1] - other[:1]
        stat = jnp.concatenate(
            [
                0.5 * (stat[:1] + other[:1]),
                stat[1:] + other[1:] + gap * gap * (0.5 * count),
            ]
        )
        count = 2 * count
    return jnp.concatenate([stat[:1], lax.rsqrt(stat[1:] / count + 1e-05)])


def merge_means(sums, count):
    for bit in bits_of("tm"):
        sums = sums + swap(sums, "tm", bit)
    return sums / count


def gather_rows(value, axis, order):
    index = index_of(axis)
    value = value[(None,) * len(order)]
    for bit in order:
        other = swap(value, axis, bit)
        upper = (index // bit) % 2 == 1
        place = len(order) - bit.bit_length()
        value = jnp.concatenate(
            [jnp.where(upper, other, value), jnp.where(upper, value, other)], axis=place
        )
    return value.reshape((lax.axis_size(axis),) + value.shape[len(order) :])


def tree(value, axis, order):
    parts = {0: value}
    for bit in order:
        parts |= {offset ^ bit: swap(part, axis, bit) for offset, part in parts.items()}
    return parts


def rows_in_place(parts, axis):
    count = len(parts)
    share, width = parts[0].shape

    def body(index, *refs):
        ins, out, wide, sems = refs[:count], refs[count], refs[count + 1], refs[count + 2]
        copies = []
        for offset, ref in enumerate(ins):
            wide[offset] = ref[...].astype(F32)
            start = pl.multiple_of((index[0] ^ offset) * share, share)
            copy = pltpu.make_async_copy(
                wide.at[offset], out.at[pl.ds(start, share), :], sems.at[offset]
            )
            copy.start()
            copies.append(copy)
        for copy in copies:
            copy.wait()

    space = pl.BlockSpec(memory_space=pltpu.MemorySpace.VMEM)
    return pl.pallas_call(
        body,
        out_shape=jax.ShapeDtypeStruct((count * share, width), F32),
        in_specs=[pl.BlockSpec(memory_space=pltpu.MemorySpace.SMEM)] + [space] * count,
        out_specs=pl.BlockSpec(memory_space=pl.ANY),
        scratch_shapes=[
            pltpu.VMEM((count, share, width), F32),
            pltpu.SemaphoreType.DMA((count,)),
        ],
        compiler_params=pltpu.CompilerParams(vmem_limit_bytes=56 * 1024 * 1024),
    )(index_of(axis).astype(jnp.int32).reshape(1), *[parts[o] for o in range(count)])


def gather_wide(value, axis, order):
    if value.shape[0] % 16 == 0:
        return rows_in_place(tree(value, axis, order), axis)
    rows = gather_rows(value, axis, order)
    return rows.reshape(rows.shape[0] * rows.shape[1], rows.shape[2]).astype(F32)


class Halving:
    def __init__(self, value, axis, order):
        self.axis, self.order = axis, list(order)
        self.left = sorted(order, reverse=True)
        self.value = value.reshape((2,) * len(order) + value.shape[1:])
        self.give = None

    def split(self):
        bit = self.order.pop(0)
        place = self.left.index(bit)
        self.left.remove(bit)
        mine = (index_of(self.axis) // bit) % 2
        self.bit = bit
        self.give = lax.dynamic_index_in_dim(self.value, 1 - mine, place, keepdims=False)
        self.give = self.give.astype(BF16)
        self.value = lax.dynamic_index_in_dim(self.value, mine, place, keepdims=False)

    def join(self):
        got = swap(self.give, self.axis, self.bit)
        self.value = self.value.astype(F32) + got.astype(F32)
        self.give = None


def together(items, *others):
    fixed = lax.optimization_barrier((tuple(item.give for item in items), others))
    for item, give in zip(items, fixed[0]):
        item.give = give
    return fixed[1]


def orders(axis):
    bits = bits_of(axis)
    return bits, bits[1:] + bits[:1]


def local(frames, query, keys, values, norm_gain, conv_gain, w_glu, taps, w_out, cotangent):
    groups = lax.axis_size("tm")
    copies = lax.axis_size("dp")
    mine = index_of("tm")
    rows, width = frames.shape[1:]
    length = rows * groups
    block = width // groups
    share = block // copies
    tm_bits = bits_of("tm")
    offsets = list(range(groups))
    near, far = orders("dp")

    def columns(arr, owner, low=0):
        return lax.dynamic_slice_in_dim(arr, owner * block + low, block, arr.ndim - 1)

    norm_all = jnp.concatenate([columns(norm_gain[None], mine ^ o) for o in offsets])
    conv_own = columns(conv_gain[None], mine)
    taps_own = columns(taps, mine)

    def glu_columns(arr, owner):
        return jnp.concatenate([columns(arr, owner), columns(arr, owner, width)], axis=1)

    distant = [o for o in offsets if o > 1]
    if distant:
        place = index_of("dp") * share
        w_share = lax.dynamic_slice_in_dim(w_glu, place, share, 0)
        fetched = jnp.stack([swap(glu_columns(w_share, mine ^ o), "tm", o) for o in distant])

    def exchange(arrays):
        blocks = []
        for m in range(groups):
            piece = jnp.concatenate([columns(arr, mine ^ m) for arr in arrays])
            blocks.append(piece if m == 0 else swap(piece, "tm", m))
        return blocks

    blocks = exchange([query, keys, values])
    residual = exchange([frames])
    if distant:
        fetched, blocks[-1] = lax.optimization_barrier((fetched, blocks[-1]))
    w_parts = {0: glu_columns(w_glu, mine), 1: swap(glu_columns(w_glu, mine ^ 1), "tm", 1)}

    w_far = {}
    if distant and share % 16 == 0:
        w_far = tree(fetched, "dp", near[::-1])
        early = {o: w_far[o] for o in w_far if o.bit_count() == 1 and o > 1}
        early, blocks[-1] = lax.optimization_barrier((early, blocks[-1]))
        w_far = w_far | early
    elif distant:
        spread = gather_rows(fetched, "dp", near[::-1])
        for i, offset in enumerate(distant):
            w_parts[offset] = spread[:, i].reshape(block, 2 * block)

    cot, blocks[-1] = lax.optimization_barrier((cotangent[0], blocks[-1]))
    mixed, stat_u = attend(mine, blocks, residual, width // HEADS)
    stat_u = merge_moments(stat_u, block)
    parts = {0: mixed}
    for bit in reversed(tm_bits):
        parts |= {offset ^ bit: swap(part, "tm", bit) for offset, part in parts.items()}
    cot_all = gather_rows(cot, "tm", tm_bits[::-1]).reshape(length, width)
    d_s = lax.dot_general(cot_all, w_out, (((1,), (1,)), ((), ())), preferred_element_type=F32)

    last = parts[groups - 1]
    d_s, parts[groups - 1] = lax.optimization_barrier((d_s, last))
    u_all, p_own, y_rows, z_rows, stat_z = gate(
        [parts[o] for o in offsets],
        stat_u,
        norm_all,
        list(w_parts.values()),
        [w_far[o] for o in range(len(w_far))],
        taps_own,
    )
    stat_z = merge_moments(stat_z, block)
    s_turned, zhat, e_rows, sums = swish(z_rows, stat_z, conv_own, d_s)
    contract = (((0,), (0,)), ((), ()))
    middle = width // 2
    out_term = jnp.dot(s_turned, cot_all, preferred_element_type=F32)
    out_term = out_term.reshape(copies, share, width)
    outs = [Halving(out_term[..., :middle], "dp", near), Halving(out_term[..., middle:], "dp", far)]
    steps = len(near)
    for item in outs:
        item.split()
    (sums,) = together(outs, sums)
    for item in outs:
        item.join()

    means = merge_means(sums, width)
    d_p, d_z = ungate(e_rows, zhat, stat_z, means, p_own, taps_own)
    if steps > 1:
        for item in outs:
            item.split()
        (d_p,) = together(outs, d_p)
        for item in outs:
            item.join()

    glu_term = lax.dot_general(u_all, d_p, contract, preferred_element_type=F32)
    glu_term = glu_term.reshape(groups, copies, share, 2 * block).transpose(1, 0, 2, 3)
    glus = [Halving(glu_term[..., :block], "dp", near), Halving(glu_term[..., block:], "dp", far)]
    for item in glus:
        item.split()
    d_z, y_rows = together(glus, d_z, y_rows)
    taps_sum = taps_gradient(d_z, y_rows, taps.shape[0])
    for item in glus:
        item.join()
    for i in range(1, steps):
        for item in glus:
            item.split()
        (taps_sum,) = together(glus[:1], taps_sum)
        if i + 1 < steps:
            for item in outs:
                item.split()
            together(glus[:1] + outs)
            for item in outs:
                item.join()
        taps_sum = taps_sum + swap(taps_sum, "dp", near[i - 1])
        for item in glus:
            item.join()

    pieces = []
    for item in glus:
        part = item.value.astype(BF16)
        got = jnp.stack([part[0]] + [swap(part[o], "tm", o) for o in offsets[1:]])
        ordered = [
            lax.dynamic_index_in_dim(got, mine ^ g, 0, keepdims=False) for g in range(groups)
        ]
        pieces += ordered
    out_piece = jnp.concatenate([item.value.astype(BF16) for item in outs], axis=1)
    glu_piece = jnp.concatenate(pieces, axis=1)
    (taps_sum, glu_piece) = lax.optimization_barrier((taps_sum, glu_piece))
    taps_sum = taps_sum + swap(taps_sum, "dp", near[-1])
    out_grad = gather_wide(out_piece, "dp", far[::-1])
    glu_grad = gather_wide(glu_piece, "dp", near[::-1])
    return (glu_grad, taps_sum, out_grad)


def solution(mesh):
    return jax.shard_map(
        local,
        mesh=mesh,
        in_specs=(
            P("dp", "tm", None),
            P("dp", "tm", None),
            P("dp", "tm", None),
            P("dp", "tm", None),
            P(),
            P(),
            P("tm", None),
            P(),
            P("tm", None),
            P("dp", "tm", None),
        ),
        out_specs=(P("tm", None), P(None, "tm"), P("tm", None)),
        check_vma=False,
    )
```

```python
import jax
import jax.numpy as jnp
from jax import lax
from jax.experimental import pallas as pl
from jax.experimental.pallas import tpu as pltpu
from jax.sharding import PartitionSpec as P


HEADS = 16
LANES = 128
F32 = jnp.float32
BF16 = jnp.bfloat16


def bits_of(size):
    return [1 << i for i in range(size.bit_length() - 1)]


def swap(value, axis, offset):
    size = lax.axis_size(axis)
    return lax.ppermute(value, axis, [(i, i ^ offset) for i in range(size)])


def index_of(axis):
    return lax.axis_index(axis).astype(jnp.uint32)


def tile_width(block):
    return LANES if block % LANES == 0 else block


def as_row(column):
    return jnp.broadcast_to(column, (column.shape[0], LANES)).T[:1]


def as_column(row):
    return jnp.broadcast_to(row, (LANES, row.shape[1])).T[:, :1]


def moments(value):
    mean = jnp.mean(value, axis=1, keepdims=True)
    centred = value - mean
    spread = jnp.sum(centred * centred, axis=1, keepdims=True)
    return centred, jnp.concatenate([as_row(mean), as_row(spread)])


def merge_moments(stats, rows, count):
    means = [stat[:1, rows] for stat in stats]
    mean = sum(means[1:], means[0]) / len(stats)
    spread = sum([stat[1:, rows] for stat in stats[1:]], stats[0][1:, rows])
    gaps = [(m - mean) * (m - mean) for m in means]
    spread = spread + count * sum(gaps[1:], gaps[0])
    return mean, lax.rsqrt(spread / (count * len(stats)) + 1e-05)


def call(body, outs, args, scratch=(), scalars=()):
    space = pl.BlockSpec(memory_space=pltpu.MemorySpace.VMEM)
    scalar = pl.BlockSpec(memory_space=pltpu.MemorySpace.SMEM)
    return pl.pallas_call(
        body,
        out_shape=[jax.ShapeDtypeStruct(shape, dtype) for shape, dtype in outs],
        in_specs=[scalar] * len(scalars) + [space] * len(args),
        out_specs=[space] * len(outs),
        scratch_shapes=list(scratch),
        compiler_params=pltpu.CompilerParams(vmem_limit_bytes=56 * 1024 * 1024),
    )(*scalars, *args)


def attend(mine, blocks, residual, head_dim):
    groups = len(blocks)
    rows, width = blocks[0].shape[1:]
    length = groups * rows
    scale = head_dim ** (-0.5)

    def body(index, *refs):
        parts, rest, (mixed, stat) = refs[:groups], refs[groups : 2 * groups], refs[2 * groups :]
        outs = [[] for _ in parts]
        for low in range(0, width, head_dim):
            cols = slice(low, low + head_dim)
            k = jnp.concatenate([part[1, :, cols] for part in parts])
            v = jnp.concatenate([part[2, :, cols] for part in parts])
            for m, part in enumerate(parts):
                scores = lax.dot_general(
                    part[0, :, cols], k, (((1,), (1,)), ((), ())), preferred_element_type=F32
                )
                scores = scores * scale
                expo = jnp.exp(scores - jnp.max(scores, axis=1, keepdims=True))
                total = jnp.sum(expo, axis=1, keepdims=True)
                summed = jnp.dot(expo.astype(BF16), v, preferred_element_type=F32)
                outs[m].append((summed / total).astype(BF16))
        for m, part in enumerate(rest):
            start = pl.multiple_of((index[0] ^ m) * rows, rows)
            value = part[0].astype(F32) + jnp.concatenate(outs[m], axis=1).astype(F32)
            centred, stat[:, pl.ds(start, rows)] = moments(value)
            mixed[pl.ds(start, rows), :] = centred.astype(BF16)

    return call(
        body, [((length, width), BF16), ((2, length), F32)],
        [*blocks, *residual],
        scalars=[mine.astype(jnp.int32).reshape(1)],
    )


def fill(padded, half, length, width, read):
    tile = tile_width(width)
    for i in range(width // tile):
        padded[i, :half] = jnp.zeros((half, tile), F32)
        padded[i, half + length :] = jnp.zeros((half, tile), F32)
        for low in range(0, length, LANES):
            padded[i, half + low : half + low + LANES] = read(low, i * tile, tile)


def convolve(padded, taps, length, width, places, write, chunk=64):
    tile = tile_width(width)
    for i in range(width // tile):
        cols = slice(i * tile, (i + 1) * tile)

        def step(j, carry, i=i, cols=cols):
            start = pl.multiple_of(j * chunk, chunk)
            total = jnp.zeros((chunk, tile), F32)
            for t, place in enumerate(places):
                total = total + taps[t : t + 1, cols] * padded[i, pl.ds(start + place, chunk)]
            write(start, chunk, cols, total)
            return carry

        lax.fori_loop(0, length // chunk, step, 0)


def gate(parts, stats, gain, w_near, w_far, taps):
    length, block = parts[0].shape
    count = len(parts)
    kernel = taps.shape[0]
    half = kernel // 2
    tile = tile_width(block)

    close, copies = len(w_near), len(w_far)

    def body(index, *refs):
        ins, ws, far = refs[:count], list(refs[count : count + close]), refs[count + close :]
        far, refs = far[:copies], far[copies:]
        stat_refs, refs = refs[:count], refs[count:]
        gain_ref, taps_ref, u_ref, p_ref, y_ref, z_ref, stat, padded = refs[:8]
        if copies:
            whole = refs[8]
            share = far[0].shape[1]
            for offset, ref in enumerate(far):
                start = pl.multiple_of((index[0] ^ offset) * share, share)
                for m in range(count - close):
                    whole[m, pl.ds(start, share), :] = ref[m]
            ws += [whole.at[m] for m in range(count - close)]
        for low in range(0, length, LANES):
            rows = slice(low, low + LANES)
            mean, inv = merge_moments(stat_refs, rows, block)
            shifts = [as_column(ref[:1, rows] - mean) for ref in stat_refs]
            inv = as_column(inv)
            p = jnp.zeros((LANES, 2 * block), F32)
            for m, (part, w) in enumerate(zip(ins, ws)):
                u = (part[rows].astype(F32) + shifts[m]) * inv * gain_ref[m : m + 1]
                u = u.astype(BF16)
                u_ref[rows, m * block : (m + 1) * block] = u
                p = p + jnp.dot(u, w[...], preferred_element_type=F32)
            p_ref[rows] = p
            y_ref[rows] = (p[:, :block] * jax.nn.sigmoid(p[:, block:])).astype(BF16)
        fill(
            padded,
            half,
            length,
            block,
            lambda low, col, size: y_ref[low : low + LANES, col : col + size].astype(F32),
        )

        def write(start, chunk, cols, total):
            z_ref[pl.ds(start, chunk), cols] = total

        convolve(padded, taps_ref, length, block, range(kernel), write)
        for low in range(0, length, LANES):
            rows = slice(low, low + LANES)
            stat[:, rows] = moments(z_ref[rows])[1]

    return call(
        body,
        [
            ((length, count * block), BF16),
            ((length, 2 * block), F32),
            ((length, block), BF16),
            ((length, block), F32),
            ((2, length), F32),
        ],
        [*parts, *w_near, *w_far, *stats, gain, taps],
        [pltpu.VMEM((block // tile, length + 2 * half, tile), F32)]
        + ([pltpu.VMEM((count - close, block, 2 * block), BF16)] if copies else []),
        scalars=[index_of("dp").astype(jnp.int32).reshape(1)],
    )


def swish(z, stats, gain, d_s):
    length, block = z.shape
    count = len(stats)

    def body(z_ref, gain_ref, ds_ref, *refs):
        stat_refs, (s_ref, zhat_ref, e_ref, inv_ref, sums) = refs[:count], refs[count:]
        for low in range(0, length, LANES):
            rows = slice(low, low + LANES)
            mean, inv = merge_moments(stat_refs, rows, block)
            inv_ref[:, rows] = inv
            zhat = (z_ref[rows] - as_column(mean)) * as_column(inv)
            n = zhat * gain_ref[...]
            sgate = jax.nn.sigmoid(n)
            s_ref[:, rows] = (n * sgate).T.astype(BF16)
            e = ds_ref[rows] * sgate * (1.0 + n * (1.0 - sgate)) * gain_ref[...]
            zhat_ref[rows] = zhat
            e_ref[rows] = e
            both = [jnp.sum(e, axis=1, keepdims=True), jnp.sum(e * zhat, axis=1, keepdims=True)]
            sums[:, rows] = jnp.concatenate([as_row(both[0]), as_row(both[1])])

    return call(
        body,
        [
            ((block, length), BF16),
            ((length, block), F32),
            ((length, block), F32),
            ((1, length), F32),
            ((2, length), F32),
        ],
        [z, gain, d_s, *stats],
    )


def ungate(e, zhat, inv, sums, p, taps):
    length, block = e.shape
    kernel = taps.shape[0]
    half = kernel // 2
    tile = tile_width(block)

    count = len(sums)

    def body(e_ref, zhat_ref, inv_ref, p_ref, taps_ref, *refs):
        sum_refs, (dp_ref, dz_ref, padded) = refs[:count], refs[count:]
        for low in range(0, length, LANES):
            rows = slice(low, low + LANES)
            means = sum([ref[:, rows] for ref in sum_refs[1:]], sum_refs[0][:, rows])
            means = means / (block * count)
            mean, mean_z = as_column(means[:1]), as_column(means[1:])
            d_z = (e_ref[rows] - mean - zhat_ref[rows] * mean_z) * as_column(inv_ref[:, rows])
            dz_ref[rows] = d_z.astype(BF16)
        fill(
            padded,
            half,
            length,
            block,
            lambda low, col, size: dz_ref[low : low + LANES, col : col + size].astype(F32),
        )

        def write(start, chunk, cols, total):
            rows = pl.ds(start, chunk)
            first = p_ref[rows, cols]
            sig = jax.nn.sigmoid(p_ref[rows, slice(block + cols.start, block + cols.stop)])
            dp_ref[rows, cols] = (total * sig).astype(BF16)
            dp_ref[rows, slice(block + cols.start, block + cols.stop)] = (
                total * first * sig * (1.0 - sig)
            ).astype(BF16)

        convolve(
            padded, taps_ref, length, block, [2 * half - t for t in range(kernel)], write
        )

    return call(
        body,
        [((length, 2 * block), BF16), ((length, block), BF16)],
        [e, zhat, inv, p, taps, *sums],
        [pltpu.VMEM((block // tile, length + 2 * half, tile), F32)],
    )


def taps_gradient(d_z, y, kernel):
    length, block = y.shape
    half = kernel // 2
    tile = tile_width(block)
    group = 8

    def body(dz_ref, y_ref, out, dz_all, y_pad):
        for ref, padded in ((dz_ref, dz_all), (y_ref, y_pad)):
            fill(
                padded,
                half,
                length,
                block,
                lambda low, col, size, ref=ref: ref[low : low + LANES, col : col + size].astype(F32),
            )
        for i in range(block // tile):

            def step(j, sums, i=i):
                start = pl.multiple_of(j * group, group)
                value = dz_all[i, pl.ds(start + half, group)]
                return tuple(
                    total + value * y_pad[i, pl.ds(start + t, group)]
                    for t, total in enumerate(sums)
                )

            zero = jnp.zeros((group, tile), F32)
            sums = lax.fori_loop(0, length // group, step, (zero,) * kernel)
            out[:, i * tile : (i + 1) * tile] = jnp.concatenate(
                [jnp.sum(total, axis=0, keepdims=True) for total in sums]
            )

    pad = pltpu.VMEM((block // tile, length + 2 * half, tile), F32)
    return call(body, [((kernel, block), F32)], [d_z, y], [pad, pad])[0]


def gather_rows(value, axis, order):
    index = index_of(axis)
    value = value[(None,) * len(order)]
    for bit in order:
        other = swap(value, axis, bit)
        upper = (index // bit) % 2 == 1
        place = len(order) - bit.bit_length()
        value = jnp.concatenate(
            [jnp.where(upper, other, value), jnp.where(upper, value, other)], axis=place
        )
    return value.reshape((lax.axis_size(axis),) + value.shape[len(order) :])


def tree(value, axis, order):
    parts = {0: value}
    for bit in order:
        parts |= {offset ^ bit: swap(part, axis, bit) for offset, part in parts.items()}
    return parts


def rows_in_place(jobs, widths, axis, into=()):
    count, given = len(jobs), len(into)
    total = lax.axis_size(axis) * jobs[0][0].shape[0]

    def body(index, *refs):
        ins = refs[:count]
        outs = refs[count + given : count + given + len(widths)]
        wides, sem = refs[count + given + len(widths) : -1], refs[-1]
        copies = []
        for ref, wide, (_, offset, spans) in zip(ins, wides, jobs):
            share = ref.shape[0]
            wide[...] = ref[...].astype(F32)
            start = pl.multiple_of((index[0] ^ offset) * share, share)
            for which, low, high, place in spans:
                copy = pltpu.make_async_copy(
                    wide.at[:, low:high],
                    outs[which].at[pl.ds(start, share), place : place + high - low],
                    sem.at[len(copies)],
                )
                copy.start()
                copies.append(copy)
        for copy in copies:
            copy.wait()

    space = pl.BlockSpec(memory_space=pltpu.MemorySpace.VMEM)
    whole = pl.BlockSpec(memory_space=pl.ANY)
    return pl.pallas_call(
        body,
        out_shape=[jax.ShapeDtypeStruct((total, width), F32) for width in widths],
        in_specs=[pl.BlockSpec(memory_space=pltpu.MemorySpace.SMEM)]
        + [space] * count
        + [whole] * given,
        out_specs=[whole] * len(widths),
        scratch_shapes=[pltpu.VMEM(array.shape, F32) for array, _, _ in jobs]
        + [pltpu.SemaphoreType.DMA((sum(len(spans) for _, _, spans in jobs),))],
        input_output_aliases={count + 1 + j: j for j in range(given)},
        compiler_params=pltpu.CompilerParams(vmem_limit_bytes=56 * 1024 * 1024),
    )(index_of(axis).astype(jnp.int32).reshape(1), *[job[0] for job in jobs], *into)


def gather_both(glu, out, near, far):
    share, wide = glu.shape
    width = out.shape[1]
    cut = width // 2
    both = jnp.concatenate([glu, out[:, :cut]], axis=1)
    middle = (wide + cut) // 2
    if share % 16 == 0 and middle % LANES == 0 and middle <= wide:
        one = tree(both[:, :middle], "dp", near)
        two = tree(both[:, middle:], "dp", near)
        short = tree(out[:, cut:], "dp", far)
        spans = [(0, 0, middle, 0)], [
            (0, 0, wide - middle, middle),
            (1, wide - middle, middle, 0),
        ]
        jobs = [(part, o, spans[i]) for i, parts in enumerate((one, two)) for o, part in parts.items()]
        jobs += [(part, o, [(1, 0, cut, cut)]) for o, part in short.items()]
        first = [0] + near[:2]
        early = [job for job in jobs[: 2 * len(one)] if job[1] in first]
        early += [job for job in jobs[2 * len(one) :] if job[1] in (0, far[0])]
        rest = [job for job in jobs if not any(job is other for other in early)]
        into = rows_in_place(early, (wide, width), "dp")
        return rows_in_place(rest, (wide, width), "dp", into)
    long, short = both, out[:, cut:]
    long = gather_rows(long, "dp", near).reshape(-1, wide + cut).astype(F32)
    short = gather_rows(short, "dp", far).reshape(-1, width - cut).astype(F32)
    return long[:, :wide], jnp.concatenate([long[:, wide:], short], axis=1)


class Halving:
    def __init__(self, value, axis, order):
        self.axis, self.order = axis, list(order)
        self.left = sorted(order, reverse=True)
        self.value = value.reshape((2,) * len(order) + value.shape[1:])
        self.give = None

    def split(self):
        bit = self.order.pop(0)
        place = self.left.index(bit)
        self.left.remove(bit)
        mine = (index_of(self.axis) // bit) % 2
        self.bit = bit
        self.give = lax.dynamic_index_in_dim(self.value, 1 - mine, place, keepdims=False)
        self.give = self.give.astype(BF16)
        self.value = lax.dynamic_index_in_dim(self.value, mine, place, keepdims=False)

    def join(self):
        got = swap(self.give, self.axis, self.bit)
        self.value = self.value.astype(F32) + got.astype(F32)
        self.give = None


def together(items, *others):
    fixed = lax.optimization_barrier((tuple(item.give for item in items), others))
    for item, give in zip(items, fixed[0]):
        item.give = give
    return fixed[1]


def orders(size):
    bits = bits_of(size)
    return bits, bits[1:] + bits[:1]


def whole_step(frames, query, keys, values, norm_gain, conv_gain, w_glu, taps, w_out, cotangent):
    groups = lax.axis_size("tm")
    copies = lax.axis_size("dp")
    mine = index_of("tm")
    rows, width = frames.shape[1:]
    length = rows * groups
    block = width // groups
    share = block // copies
    tm_bits = bits_of(lax.axis_size("tm"))
    offsets = list(range(groups))
    near, far = orders(lax.axis_size("dp"))

    def columns(arr, owner, low=0):
        return lax.dynamic_slice_in_dim(arr, owner * block + low, block, arr.ndim - 1)

    norm_all = jnp.concatenate([columns(norm_gain[None], mine ^ o) for o in offsets])
    conv_own = columns(conv_gain[None], mine)
    taps_own = columns(taps, mine)

    def glu_columns(arr, owner):
        return jnp.concatenate([columns(arr, owner), columns(arr, owner, width)], axis=1)

    distant = [o for o in offsets if o > 1]
    if distant:
        place = index_of("dp") * share
        w_share = lax.dynamic_slice_in_dim(w_glu, place, share, 0)
        fetched = jnp.stack([swap(glu_columns(w_share, mine ^ o), "tm", o) for o in distant])

    def exchange(arrays):
        blocks = []
        for m in range(groups):
            piece = jnp.concatenate([columns(arr, mine ^ m) for arr in arrays])
            blocks.append(piece if m == 0 else swap(piece, "tm", m))
        return blocks

    blocks = exchange([query, keys, values])
    residual = exchange([frames])
    w_parts = {0: glu_columns(w_glu, mine), 1: swap(glu_columns(w_glu, mine ^ 1), "tm", 1)}

    w_far = {}
    if distant and share % 16 == 0:
        w_far = tree(fetched, "dp", near[::-1])
    elif distant:
        spread = gather_rows(fetched, "dp", near[::-1])
        for i, offset in enumerate(distant):
            w_parts[offset] = spread[:, i].reshape(block, 2 * block)

    mixed, stat_u = attend(mine, blocks, residual, width // HEADS)
    stats_u = tree(stat_u, "tm", tm_bits)
    parts = {0: mixed}
    for bit in reversed(tm_bits):
        parts |= {offset ^ bit: swap(part, "tm", bit) for offset, part in parts.items()}
    cot_all = gather_rows(cotangent[0], "tm", tm_bits[::-1]).reshape(length, width)
    d_s = lax.dot_general(cot_all, w_out, (((1,), (1,)), ((), ())), preferred_element_type=F32)

    last = parts[groups - 1]
    d_s, parts[groups - 1] = lax.optimization_barrier((d_s, last))
    u_all, p_own, y_rows, z_rows, stat_z = gate(
        [parts[o] for o in offsets],
        [stats_u[o] for o in offsets],
        norm_all,
        list(w_parts.values()),
        [w_far[o] for o in range(len(w_far))],
        taps_own,
    )
    stats_z = tree(stat_z, "tm", tm_bits)
    s_turned, zhat, e_rows, inv, sums = swish(z_rows, list(stats_z.values()), conv_own, d_s)
    contract = (((0,), (0,)), ((), ()))
    middle = width // 2
    out_term = jnp.dot(s_turned, cot_all, preferred_element_type=F32)
    out_term = out_term.reshape(copies, share, width)
    outs = [Halving(out_term[..., :middle], "dp", near), Halving(out_term[..., middle:], "dp", far)]
    steps = len(near)
    for item in outs:
        item.split()
    (sums,) = together(outs, sums)
    for item in outs:
        item.join()

    sums = list(tree(sums, "tm", tm_bits).values())
    d_p, d_z = ungate(e_rows, zhat, inv, sums, p_own, taps_own)
    if steps > 1:
        for item in outs:
            item.split()
        (d_p,) = together(outs, d_p)
        for item in outs:
            item.join()

    glu_term = lax.dot_general(u_all, d_p, contract, preferred_element_type=F32)
    glu_term = glu_term.reshape(groups, copies, share, 2 * block).transpose(1, 0, 2, 3)
    glus = [Halving(glu_term[..., :block], "dp", near), Halving(glu_term[..., block:], "dp", far)]
    for item in glus:
        item.split()
    d_z, y_rows = together(glus, d_z, y_rows)
    taps_sum = taps_gradient(d_z, y_rows, taps.shape[0])
    for item in glus:
        item.join()
    for i in range(1, steps):
        for item in glus:
            item.split()
        (taps_sum,) = together(glus[:1], taps_sum)
        if i + 1 < steps:
            for item in outs:
                item.split()
            together(glus[:1] + outs)
            for item in outs:
                item.join()
        taps_sum = taps_sum + swap(taps_sum, "dp", near[i - 1])
        for item in glus:
            item.join()

    pieces = []
    for item in glus:
        part = item.value.astype(BF16)
        got = jnp.stack([part[0]] + [swap(part[o], "tm", o) for o in offsets[1:]])
        ordered = [
            lax.dynamic_index_in_dim(got, mine ^ g, 0, keepdims=False) for g in range(groups)
        ]
        pieces += ordered
    out_piece = jnp.concatenate([item.value.astype(BF16) for item in outs], axis=1)
    glu_piece = jnp.concatenate(pieces, axis=1)
    (taps_sum, glu_piece) = lax.optimization_barrier((taps_sum, glu_piece))
    taps_sum = taps_sum + swap(taps_sum, "dp", near[-1])
    glu_grad, out_grad = gather_both(glu_piece, out_piece, near[::-1], far[::-1])
    return (glu_grad, taps_sum, out_grad)


def solution(mesh):
    return jax.shard_map(
        whole_step,
        mesh=mesh,
        in_specs=(
            P("dp", "tm", None),
            P("dp", "tm", None),
            P("dp", "tm", None),
            P("dp", "tm", None),
            P(),
            P(),
            P("tm", None),
            P(),
            P("tm", None),
            P("dp", "tm", None),
        ),
        out_specs=(P("tm", None), P(None, "tm"), P("tm", None)),
        check_vma=False,
    )
```

```python
import jax
import jax.numpy as jnp
from jax import lax
from jax.experimental import pallas as pl
from jax.experimental.pallas import tpu as pltpu
from jax.sharding import PartitionSpec as P


HEADS = 16
LANES = 128
ATTEND_ROWS = 512
F32 = jnp.float32
BF16 = jnp.bfloat16


def bits_of(size):
    return [1 << i for i in range(size.bit_length() - 1)]


def swap(value, axis, offset):
    size = lax.axis_size(axis)
    return lax.ppermute(value, axis, [(i, i ^ offset) for i in range(size)])


def index_of(axis):
    return lax.axis_index(axis).astype(jnp.uint32)


def tile_width(block):
    return LANES if block % LANES == 0 else block


def as_row(column):
    return jnp.broadcast_to(column, (column.shape[0], LANES)).T[:1]


def as_column(row):
    return jnp.broadcast_to(row, (LANES, row.shape[1])).T[:, :1]


def moments(value):
    mean = jnp.mean(value, axis=1, keepdims=True)
    centred = value - mean
    spread = jnp.sum(centred * centred, axis=1, keepdims=True)
    return centred, jnp.concatenate([as_row(mean), as_row(spread)])


def merge_moments(stats, rows, count):
    means = [stat[:1, rows] for stat in stats]
    mean = sum(means[1:], means[0]) / len(stats)
    spread = sum([stat[1:, rows] for stat in stats[1:]], stats[0][1:, rows])
    gaps = [(m - mean) * (m - mean) for m in means]
    spread = spread + count * sum(gaps[1:], gaps[0])
    return mean, lax.rsqrt(spread / (count * len(stats)) + 1e-05)


def call(body, outs, args, scratch=(), scalars=()):
    space = pl.BlockSpec(memory_space=pltpu.MemorySpace.VMEM)
    scalar = pl.BlockSpec(memory_space=pltpu.MemorySpace.SMEM)
    return pl.pallas_call(
        body,
        out_shape=[jax.ShapeDtypeStruct(shape, dtype) for shape, dtype in outs],
        in_specs=[scalar] * len(scalars) + [space] * len(args),
        out_specs=[space] * len(outs),
        scratch_shapes=list(scratch),
        compiler_params=pltpu.CompilerParams(vmem_limit_bytes=56 * 1024 * 1024),
    )(*scalars, *args)


def attend(mine, blocks, residual, head_dim):
    groups = len(blocks)
    rows, width = blocks[0].shape[1:]
    length = groups * rows
    scale = head_dim ** (-0.5)

    def body(index, *refs):
        parts, rest, (mixed, stat) = refs[:groups], refs[groups : 2 * groups], refs[2 * groups :]
        outs = []
        for low in range(0, width, head_dim):
            cols = slice(low, low + head_dim)
            q, k, v = [jnp.concatenate([part[i, :, cols] for part in parts]) for i in range(3)]
            heads = []
            for first in range(0, length, ATTEND_ROWS):
                scores = lax.dot_general(
                    q[first : first + ATTEND_ROWS],
                    k,
                    (((1,), (1,)), ((), ())),
                    preferred_element_type=F32,
                )
                scores = scores * scale
                expo = jnp.exp(scores - jnp.max(scores, axis=1, keepdims=True))
                total = jnp.sum(expo, axis=1, keepdims=True)
                summed = jnp.dot(expo.astype(BF16), v, preferred_element_type=F32)
                heads.append((summed / total).astype(BF16))
            outs.append(jnp.concatenate(heads))
        attention = jnp.concatenate(outs, axis=1)
        for m, part in enumerate(rest):
            start = pl.multiple_of((index[0] ^ m) * rows, rows)
            value = part[0].astype(F32) + attention[m * rows : (m + 1) * rows].astype(F32)
            centred, stat[:, pl.ds(start, rows)] = moments(value)
            mixed[pl.ds(start, rows), :] = centred.astype(BF16)

    return call(
        body, [((length, width), BF16), ((2, length), F32)],
        [*blocks, *residual],
        scalars=[mine.astype(jnp.int32).reshape(1)],
    )


def fill(padded, half, length, width, read):
    tile = tile_width(width)
    for i in range(width // tile):
        padded[i, :half] = jnp.zeros((half, tile), F32)
        padded[i, half + length :] = jnp.zeros((half, tile), F32)
        for low in range(0, length, LANES):
            padded[i, half + low : half + low + LANES] = read(low, i * tile, tile)


def convolve(padded, taps, length, width, places, write, chunk=64):
    tile = tile_width(width)
    for i in range(width // tile):
        cols = slice(i * tile, (i + 1) * tile)

        def step(j, carry, i=i, cols=cols):
            start = pl.multiple_of(j * chunk, chunk)
            total = jnp.zeros((chunk, tile), F32)
            for t, place in enumerate(places):
                total = total + taps[t : t + 1, cols] * padded[i, pl.ds(start + place, chunk)]
            write(start, chunk, cols, total)
            return carry

        lax.fori_loop(0, length // chunk, step, 0)


def gate(parts, stats, gain, w_near, w_far, taps):
    length, block = parts[0].shape
    count = len(parts)
    kernel = taps.shape[0]
    half = kernel // 2
    tile = tile_width(block)

    close, copies = len(w_near), len(w_far)

    def body(index, *refs):
        ins, ws, far = refs[:count], list(refs[count : count + close]), refs[count + close :]
        far, refs = far[:copies], far[copies:]
        stat_refs, refs = refs[:count], refs[count:]
        gain_ref, taps_ref, u_ref, p_ref, y_ref, z_ref, stat, padded = refs[:8]
        if copies:
            whole = refs[8]
            share = far[0].shape[1]
            for offset, ref in enumerate(far):
                start = pl.multiple_of((index[0] ^ offset) * share, share)
                for m in range(count - close):
                    whole[m, pl.ds(start, share), :] = ref[m]
            ws += [whole.at[m] for m in range(count - close)]
        for low in range(0, length, LANES):
            rows = slice(low, low + LANES)
            mean, inv = merge_moments(stat_refs, rows, block)
            shifts = [as_column(ref[:1, rows] - mean) for ref in stat_refs]
            inv = as_column(inv)
            p = jnp.zeros((LANES, 2 * block), F32)
            for m, (part, w) in enumerate(zip(ins, ws)):
                u = (part[rows].astype(F32) + shifts[m]) * inv * gain_ref[m : m + 1]
                u = u.astype(BF16)
                u_ref[rows, m * block : (m + 1) * block] = u
                p = p + jnp.dot(u, w[...], preferred_element_type=F32)
            p_ref[rows] = p
            y_ref[rows] = (p[:, :block] * jax.nn.sigmoid(p[:, block:])).astype(BF16)
        fill(
            padded,
            half,
            length,
            block,
            lambda low, col, size: y_ref[low : low + LANES, col : col + size].astype(F32),
        )

        def write(start, chunk, cols, total):
            z_ref[pl.ds(start, chunk), cols] = total

        convolve(padded, taps_ref, length, block, range(kernel), write)
        for low in range(0, length, LANES):
            rows = slice(low, low + LANES)
            stat[:, rows] = moments(z_ref[rows])[1]

    return call(
        body,
        [
            ((length, count * block), BF16),
            ((length, 2 * block), F32),
            ((length, block), BF16),
            ((length, block), F32),
            ((2, length), F32),
        ],
        [*parts, *w_near, *w_far, *stats, gain, taps],
        [pltpu.VMEM((block // tile, length + 2 * half, tile), F32)]
        + ([pltpu.VMEM((count - close, block, 2 * block), BF16)] if copies else []),
        scalars=[index_of("dp").astype(jnp.int32).reshape(1)],
    )


def swish(z, stats, gain, d_s):
    length, block = z.shape
    count = len(stats)

    def body(z_ref, gain_ref, ds_ref, *refs):
        stat_refs, (s_ref, zhat_ref, e_ref, inv_ref, sums) = refs[:count], refs[count:]
        for low in range(0, length, LANES):
            rows = slice(low, low + LANES)
            mean, inv = merge_moments(stat_refs, rows, block)
            inv_ref[:, rows] = inv
            zhat = (z_ref[rows] - as_column(mean)) * as_column(inv)
            n = zhat * gain_ref[...]
            sgate = jax.nn.sigmoid(n)
            s_ref[:, rows] = (n * sgate).T.astype(BF16)
            e = ds_ref[rows] * sgate * (1.0 + n * (1.0 - sgate)) * gain_ref[...]
            zhat_ref[rows] = zhat
            e_ref[rows] = e
            both = [jnp.sum(e, axis=1, keepdims=True), jnp.sum(e * zhat, axis=1, keepdims=True)]
            sums[:, rows] = jnp.concatenate([as_row(both[0]), as_row(both[1])])

    return call(
        body,
        [
            ((block, length), BF16),
            ((length, block), F32),
            ((length, block), F32),
            ((1, length), F32),
            ((2, length), F32),
        ],
        [z, gain, d_s, *stats],
    )


def ungate(e, zhat, inv, sums, p, taps):
    length, block = e.shape
    kernel = taps.shape[0]
    half = kernel // 2
    tile = tile_width(block)

    count = len(sums)

    def body(e_ref, zhat_ref, inv_ref, p_ref, taps_ref, *refs):
        sum_refs, (dp_ref, dz_ref, padded) = refs[:count], refs[count:]
        for low in range(0, length, LANES):
            rows = slice(low, low + LANES)
            means = sum([ref[:, rows] for ref in sum_refs[1:]], sum_refs[0][:, rows])
            means = means / (block * count)
            mean, mean_z = as_column(means[:1]), as_column(means[1:])
            d_z = (e_ref[rows] - mean - zhat_ref[rows] * mean_z) * as_column(inv_ref[:, rows])
            dz_ref[rows] = d_z.astype(BF16)
        fill(
            padded,
            half,
            length,
            block,
            lambda low, col, size: dz_ref[low : low + LANES, col : col + size].astype(F32),
        )

        def write(start, chunk, cols, total):
            rows = pl.ds(start, chunk)
            first = p_ref[rows, cols]
            sig = jax.nn.sigmoid(p_ref[rows, slice(block + cols.start, block + cols.stop)])
            dp_ref[rows, cols] = (total * sig).astype(BF16)
            dp_ref[rows, slice(block + cols.start, block + cols.stop)] = (
                total * first * sig * (1.0 - sig)
            ).astype(BF16)

        convolve(
            padded, taps_ref, length, block, [2 * half - t for t in range(kernel)], write
        )

    return call(
        body,
        [((length, 2 * block), BF16), ((length, block), BF16)],
        [e, zhat, inv, p, taps, *sums],
        [pltpu.VMEM((block // tile, length + 2 * half, tile), F32)],
    )


def taps_gradient(d_z, y, kernel):
    length, block = y.shape
    half = kernel // 2
    tile = tile_width(block)
    group = 8

    def body(dz_ref, y_ref, out, dz_all, y_pad):
        for ref, padded in ((dz_ref, dz_all), (y_ref, y_pad)):
            fill(
                padded,
                half,
                length,
                block,
                lambda low, col, size, ref=ref: ref[low : low + LANES, col : col + size].astype(F32),
            )
        for i in range(block // tile):

            def step(j, sums, i=i):
                start = pl.multiple_of(j * group, group)
                value = dz_all[i, pl.ds(start + half, group)]
                return tuple(
                    total + value * y_pad[i, pl.ds(start + t, group)]
                    for t, total in enumerate(sums)
                )

            zero = jnp.zeros((group, tile), F32)
            sums = lax.fori_loop(0, length // group, step, (zero,) * kernel)
            out[:, i * tile : (i + 1) * tile] = jnp.concatenate(
                [jnp.sum(total, axis=0, keepdims=True) for total in sums]
            )

    pad = pltpu.VMEM((block // tile, length + 2 * half, tile), F32)
    return call(body, [((kernel, block), F32)], [d_z, y], [pad, pad])[0]


def gather_rows(value, axis, order):
    index = index_of(axis)
    value = value[(None,) * len(order)]
    for bit in order:
        other = swap(value, axis, bit)
        upper = (index // bit) % 2 == 1
        place = len(order) - bit.bit_length()
        value = jnp.concatenate(
            [jnp.where(upper, other, value), jnp.where(upper, value, other)], axis=place
        )
    return value.reshape((lax.axis_size(axis),) + value.shape[len(order) :])


def tree(value, axis, order):
    parts = {0: value}
    for bit in order:
        parts |= {offset ^ bit: swap(part, axis, bit) for offset, part in parts.items()}
    return parts


def rows_in_place(jobs, widths, axis, into=()):
    count, given = len(jobs), len(into)
    total = lax.axis_size(axis) * jobs[0][0].shape[0]

    def body(index, *refs):
        ins = refs[:count]
        outs = refs[count + given : count + given + len(widths)]
        wides, sem = refs[count + given + len(widths) : -1], refs[-1]
        copies = []
        for ref, wide, (_, offset, spans) in zip(ins, wides, jobs):
            share = ref.shape[0]
            wide[...] = ref[...].astype(F32)
            start = pl.multiple_of((index[0] ^ offset) * share, share)
            for which, low, high, place in spans:
                copy = pltpu.make_async_copy(
                    wide.at[:, low:high],
                    outs[which].at[pl.ds(start, share), place : place + high - low],
                    sem.at[len(copies)],
                )
                copy.start()
                copies.append(copy)
        for copy in copies:
            copy.wait()

    space = pl.BlockSpec(memory_space=pltpu.MemorySpace.VMEM)
    whole = pl.BlockSpec(memory_space=pl.ANY)
    return pl.pallas_call(
        body,
        out_shape=[jax.ShapeDtypeStruct((total, width), F32) for width in widths],
        in_specs=[pl.BlockSpec(memory_space=pltpu.MemorySpace.SMEM)]
        + [space] * count
        + [whole] * given,
        out_specs=[whole] * len(widths),
        scratch_shapes=[pltpu.VMEM(array.shape, F32) for array, _, _ in jobs]
        + [pltpu.SemaphoreType.DMA((sum(len(spans) for _, _, spans in jobs),))],
        input_output_aliases={count + 1 + j: j for j in range(given)},
        compiler_params=pltpu.CompilerParams(vmem_limit_bytes=56 * 1024 * 1024),
    )(index_of(axis).astype(jnp.int32).reshape(1), *[job[0] for job in jobs], *into)


def gather_both(glu, out, near, far):
    share, wide = glu.shape
    width = out.shape[1]
    cut = width // 2
    both = jnp.concatenate([glu, out[:, :cut]], axis=1)
    middle = (wide + cut) // 2
    if share % 16 == 0 and middle % LANES == 0 and middle <= wide:
        one = tree(both[:, :middle], "dp", near)
        two = tree(both[:, middle:], "dp", near)
        short = tree(out[:, cut:], "dp", far)
        spans = [(0, 0, middle, 0)], [
            (0, 0, wide - middle, middle),
            (1, wide - middle, middle, 0),
        ]
        jobs = [(part, o, spans[i]) for i, parts in enumerate((one, two)) for o, part in parts.items()]
        jobs += [(part, o, [(1, 0, cut, cut)]) for o, part in short.items()]
        first = [0] + near[:2]
        early = [job for job in jobs[: 2 * len(one)] if job[1] in first]
        early += [job for job in jobs[2 * len(one) :] if job[1] in (0, far[0])]
        rest = [job for job in jobs if not any(job is other for other in early)]
        into = rows_in_place(early, (wide, width), "dp")
        return rows_in_place(rest, (wide, width), "dp", into)
    long, short = both, out[:, cut:]
    long = gather_rows(long, "dp", near).reshape(-1, wide + cut).astype(F32)
    short = gather_rows(short, "dp", far).reshape(-1, width - cut).astype(F32)
    return long[:, :wide], jnp.concatenate([long[:, wide:], short], axis=1)


class Halving:
    def __init__(self, value, axis, order):
        self.axis, self.order = axis, list(order)
        self.left = sorted(order, reverse=True)
        self.value = value.reshape((2,) * len(order) + value.shape[1:])
        self.give = None

    def split(self):
        bit = self.order.pop(0)
        place = self.left.index(bit)
        self.left.remove(bit)
        mine = (index_of(self.axis) // bit) % 2
        self.bit = bit
        self.give = lax.dynamic_index_in_dim(self.value, 1 - mine, place, keepdims=False)
        self.give = self.give.astype(BF16)
        self.value = lax.dynamic_index_in_dim(self.value, mine, place, keepdims=False)

    def join(self):
        got = swap(self.give, self.axis, self.bit)
        self.value = self.value.astype(F32) + got.astype(F32)
        self.give = None


def together(items, *others):
    fixed = lax.optimization_barrier((tuple(item.give for item in items), others))
    for item, give in zip(items, fixed[0]):
        item.give = give
    return fixed[1]


def orders(size):
    bits = bits_of(size)
    return bits, bits[1:] + bits[:1]


def whole_step(frames, query, keys, values, norm_gain, conv_gain, w_glu, taps, w_out, cotangent):
    groups = lax.axis_size("tm")
    copies = lax.axis_size("dp")
    mine = index_of("tm")
    rows, width = frames.shape[1:]
    length = rows * groups
    block = width // groups
    share = block // copies
    tm_bits = bits_of(lax.axis_size("tm"))
    offsets = list(range(groups))
    near, far = orders(lax.axis_size("dp"))

    def columns(arr, owner, low=0):
        return lax.dynamic_slice_in_dim(arr, owner * block + low, block, arr.ndim - 1)

    norm_all = jnp.concatenate([columns(norm_gain[None], mine ^ o) for o in offsets])
    conv_own = columns(conv_gain[None], mine)
    taps_own = columns(taps, mine)

    def glu_columns(arr, owner):
        return jnp.concatenate([columns(arr, owner), columns(arr, owner, width)], axis=1)

    distant = [o for o in offsets if o > 1]
    if distant:
        place = index_of("dp") * share
        w_share = lax.dynamic_slice_in_dim(w_glu, place, share, 0)
        fetched = jnp.stack([swap(glu_columns(w_share, mine ^ o), "tm", o) for o in distant])

    def exchange(arrays):
        blocks = []
        for m in range(groups):
            piece = jnp.concatenate([columns(arr, mine ^ m) for arr in arrays])
            blocks.append(piece if m == 0 else swap(piece, "tm", m))
        return blocks

    blocks = exchange([query, keys, values])
    residual = exchange([frames])
    w_parts = {0: glu_columns(w_glu, mine), 1: swap(glu_columns(w_glu, mine ^ 1), "tm", 1)}

    w_far = {}
    if distant and share % 16 == 0:
        w_far = tree(fetched, "dp", near[::-1])
    elif distant:
        spread = gather_rows(fetched, "dp", near[::-1])
        for i, offset in enumerate(distant):
            w_parts[offset] = spread[:, i].reshape(block, 2 * block)

    mixed, stat_u = attend(mine, blocks, residual, width // HEADS)
    stats_u = tree(stat_u, "tm", tm_bits)
    parts = {0: mixed}
    for bit in reversed(tm_bits):
        parts |= {offset ^ bit: swap(part, "tm", bit) for offset, part in parts.items()}
    cot_all = gather_rows(cotangent[0], "tm", tm_bits[::-1]).reshape(length, width)
    d_s = lax.dot_general(cot_all, w_out, (((1,), (1,)), ((), ())), preferred_element_type=F32)

    last = parts[groups - 1]
    d_s, parts[groups - 1] = lax.optimization_barrier((d_s, last))
    u_all, p_own, y_rows, z_rows, stat_z = gate(
        [parts[o] for o in offsets],
        [stats_u[o] for o in offsets],
        norm_all,
        list(w_parts.values()),
        [w_far[o] for o in range(len(w_far))],
        taps_own,
    )
    stats_z = tree(stat_z, "tm", tm_bits)
    s_turned, zhat, e_rows, inv, sums = swish(z_rows, list(stats_z.values()), conv_own, d_s)
    contract = (((0,), (0,)), ((), ()))
    middle = width // 2
    out_term = jnp.dot(s_turned, cot_all, preferred_element_type=F32)
    out_term = out_term.reshape(copies, share, width)
    outs = [Halving(out_term[..., :middle], "dp", near), Halving(out_term[..., middle:], "dp", far)]
    steps = len(near)
    for item in outs:
        item.split()
    for item in outs:
        item.join()

    sums = list(tree(sums, "tm", tm_bits).values())
    d_p, d_z = ungate(e_rows, zhat, inv, sums, p_own, taps_own)
    if steps > 1:
        for item in outs:
            item.split()
        (d_p,) = together(outs, d_p)
        for item in outs:
            item.join()

    glu_term = lax.dot_general(u_all, d_p, contract, preferred_element_type=F32)
    glu_term = glu_term.reshape(groups, copies, share, 2 * block).transpose(1, 0, 2, 3)
    glus = [Halving(glu_term[..., :block], "dp", near), Halving(glu_term[..., block:], "dp", far)]
    for item in glus:
        item.split()
    d_z, y_rows = together(glus, d_z, y_rows)
    taps_sum = taps_gradient(d_z, y_rows, taps.shape[0])
    for item in glus:
        item.join()
    for i in range(1, steps):
        for item in glus:
            item.split()
        (taps_sum,) = together(glus[:1], taps_sum)
        if i + 1 < steps:
            for item in outs:
                item.split()
            together(glus[:1] + outs)
            for item in outs:
                item.join()
        taps_sum = taps_sum + swap(taps_sum, "dp", near[i - 1])
        for item in glus:
            item.join()

    pieces = []
    for item in glus:
        part = item.value.astype(BF16)
        got = jnp.stack([part[0]] + [swap(part[o], "tm", o) for o in offsets[1:]])
        ordered = [
            lax.dynamic_index_in_dim(got, mine ^ g, 0, keepdims=False) for g in range(groups)
        ]
        pieces += ordered
    out_piece = jnp.concatenate([item.value.astype(BF16) for item in outs], axis=1)
    glu_piece = jnp.concatenate(pieces, axis=1)
    (taps_sum, glu_piece) = lax.optimization_barrier((taps_sum, glu_piece))
    taps_sum = taps_sum + swap(taps_sum, "dp", near[-1])
    glu_grad, out_grad = gather_both(glu_piece, out_piece, near[::-1], far[::-1])
    return (glu_grad, taps_sum, out_grad)


def solution(mesh):
    return jax.shard_map(
        whole_step,
        mesh=mesh,
        in_specs=(
            P("dp", "tm", None),
            P("dp", "tm", None),
            P("dp", "tm", None),
            P("dp", "tm", None),
            P(),
            P(),
            P("tm", None),
            P(),
            P("tm", None),
            P("dp", "tm", None),
        ),
        out_specs=(P("tm", None), P(None, "tm"), P("tm", None)),
        check_vma=False,
    )
```

```python
import jax
import jax.numpy as jnp
from jax import lax
from jax.experimental import pallas as pl
from jax.experimental.pallas import tpu as pltpu
from jax.sharding import PartitionSpec as P


HEADS = 16
LANES = 128
ATTEND_ROWS = 512
F32 = jnp.float32
BF16 = jnp.bfloat16


def bits_of(size):
    return [1 << i for i in range(size.bit_length() - 1)]


def swap(value, axis, offset):
    size = lax.axis_size(axis)
    return lax.ppermute(value, axis, [(i, i ^ offset) for i in range(size)])


def index_of(axis):
    return lax.axis_index(axis).astype(jnp.uint32)


def tile_width(block):
    return LANES if block % LANES == 0 else block


def as_row(column):
    return jnp.broadcast_to(column, (column.shape[0], LANES)).T[:1]


def as_column(row):
    return jnp.broadcast_to(row, (LANES, row.shape[1])).T[:, :1]


def moments(value):
    mean = jnp.mean(value, axis=1, keepdims=True)
    centred = value - mean
    spread = jnp.sum(centred * centred, axis=1, keepdims=True)
    return centred, jnp.concatenate([as_row(mean), as_row(spread)])


def merge_moments(stats, rows, count):
    means = [stat[:1, rows] for stat in stats]
    mean = sum(means[1:], means[0]) / len(stats)
    spread = sum([stat[1:, rows] for stat in stats[1:]], stats[0][1:, rows])
    gaps = [(m - mean) * (m - mean) for m in means]
    spread = spread + count * sum(gaps[1:], gaps[0])
    return mean, lax.rsqrt(spread / (count * len(stats)) + 1e-05)


def call(body, outs, args, scratch=(), scalars=()):
    space = pl.BlockSpec(memory_space=pltpu.MemorySpace.VMEM)
    scalar = pl.BlockSpec(memory_space=pltpu.MemorySpace.SMEM)
    return pl.pallas_call(
        body,
        out_shape=[jax.ShapeDtypeStruct(shape, dtype) for shape, dtype in outs],
        in_specs=[scalar] * len(scalars) + [space] * len(args),
        out_specs=[space] * len(outs),
        scratch_shapes=list(scratch),
        compiler_params=pltpu.CompilerParams(vmem_limit_bytes=56 * 1024 * 1024),
    )(*scalars, *args)


def attend(mine, blocks, residual, head_dim):
    groups = len(blocks)
    rows, width = blocks[0].shape[1:]
    length = groups * rows
    scale = head_dim ** (-0.5)

    def body(index, *refs):
        parts, rest, (mixed, stat) = refs[:groups], refs[groups : 2 * groups], refs[2 * groups :]
        outs = []
        for low in range(0, width, head_dim):
            cols = slice(low, low + head_dim)
            q, k, v = [jnp.concatenate([part[i, :, cols] for part in parts]) for i in range(3)]
            heads = []
            for first in range(0, length, ATTEND_ROWS):
                scores = lax.dot_general(
                    q[first : first + ATTEND_ROWS],
                    k,
                    (((1,), (1,)), ((), ())),
                    preferred_element_type=F32,
                )
                scores = scores * scale
                expo = jnp.exp(scores - jnp.max(scores, axis=1, keepdims=True))
                total = jnp.sum(expo, axis=1, keepdims=True)
                summed = jnp.dot(expo.astype(BF16), v, preferred_element_type=F32)
                heads.append((summed / total).astype(BF16))
            outs.append(jnp.concatenate(heads))
        attention = jnp.concatenate(outs, axis=1)
        for m, part in enumerate(rest):
            start = pl.multiple_of((index[0] ^ m) * rows, rows)
            value = part[0].astype(F32) + attention[m * rows : (m + 1) * rows].astype(F32)
            centred, stat[:, pl.ds(start, rows)] = moments(value)
            mixed[pl.ds(start, rows), :] = centred.astype(BF16)

    return call(
        body, [((length, width), BF16), ((2, length), F32)],
        [*blocks, *residual],
        scalars=[mine.astype(jnp.int32).reshape(1)],
    )


def fill(padded, half, length, width, read):
    tile = tile_width(width)
    for i in range(width // tile):
        padded[i, :half] = jnp.zeros((half, tile), F32)
        padded[i, half + length :] = jnp.zeros((half, tile), F32)
        for low in range(0, length, LANES):
            padded[i, half + low : half + low + LANES] = read(low, i * tile, tile)


def convolve(padded, taps, length, width, places, write, chunk=128):
    tile = tile_width(width)
    for i in range(width // tile):
        cols = slice(i * tile, (i + 1) * tile)

        def step(j, carry, i=i, cols=cols):
            start = pl.multiple_of(j * chunk, chunk)
            total = jnp.zeros((chunk, tile), F32)
            for t, place in enumerate(places):
                total = total + taps[t : t + 1, cols] * padded[i, pl.ds(start + place, chunk)]
            write(start, chunk, cols, total)
            return carry

        lax.fori_loop(0, length // chunk, step, 0)


def gate(parts, stats, gain, w_near, w_far, taps):
    length, block = parts[0].shape
    count = len(parts)
    kernel = taps.shape[0]
    half = kernel // 2
    tile = tile_width(block)

    close, copies = len(w_near), len(w_far)

    def body(index, *refs):
        ins, ws, far = refs[:count], list(refs[count : count + close]), refs[count + close :]
        far, refs = far[:copies], far[copies:]
        stat_refs, refs = refs[:count], refs[count:]
        gain_ref, taps_ref, u_ref, p_ref, y_ref, z_ref, stat, padded = refs[:8]
        if copies:
            whole = refs[8]
            share = far[0].shape[1]
            for offset, ref in enumerate(far):
                start = pl.multiple_of((index[0] ^ offset) * share, share)
                for m in range(count - close):
                    whole[m, pl.ds(start, share), :] = ref[m]
            ws += [whole.at[m] for m in range(count - close)]
        for low in range(0, length, LANES):
            rows = slice(low, low + LANES)
            mean, inv = merge_moments(stat_refs, rows, block)
            shifts = [as_column(ref[:1, rows] - mean) for ref in stat_refs]
            inv = as_column(inv)
            p = jnp.zeros((LANES, 2 * block), F32)
            for m, (part, w) in enumerate(zip(ins, ws)):
                u = (part[rows].astype(F32) + shifts[m]) * inv * gain_ref[m : m + 1]
                u = u.astype(BF16)
                u_ref[rows, m * block : (m + 1) * block] = u
                p = p + jnp.dot(u, w[...], preferred_element_type=F32)
            p_ref[rows] = p
            y_ref[rows] = (p[:, :block] * jax.nn.sigmoid(p[:, block:])).astype(BF16)
        fill(
            padded,
            half,
            length,
            block,
            lambda low, col, size: y_ref[low : low + LANES, col : col + size].astype(F32),
        )

        def write(start, chunk, cols, total):
            z_ref[pl.ds(start, chunk), cols] = total

        convolve(padded, taps_ref, length, block, range(kernel), write)
        for low in range(0, length, LANES):
            rows = slice(low, low + LANES)
            stat[:, rows] = moments(z_ref[rows])[1]

    return call(
        body,
        [
            ((length, count * block), BF16),
            ((length, 2 * block), F32),
            ((length, block), BF16),
            ((length, block), F32),
            ((2, length), F32),
        ],
        [*parts, *w_near, *w_far, *stats, gain, taps],
        [pltpu.VMEM((block // tile, length + 2 * half, tile), F32)]
        + ([pltpu.VMEM((count - close, block, 2 * block), BF16)] if copies else []),
        scalars=[index_of("dp").astype(jnp.int32).reshape(1)],
    )


def swish(z, stats, gain, d_s):
    length, block = z.shape
    count = len(stats)

    def body(z_ref, gain_ref, ds_ref, *refs):
        stat_refs, (s_ref, zhat_ref, e_ref, inv_ref, sums) = refs[:count], refs[count:]
        for low in range(0, length, LANES):
            rows = slice(low, low + LANES)
            mean, inv = merge_moments(stat_refs, rows, block)
            inv_ref[:, rows] = inv
            zhat = (z_ref[rows] - as_column(mean)) * as_column(inv)
            n = zhat * gain_ref[...]
            sgate = jax.nn.sigmoid(n)
            s_ref[:, rows] = (n * sgate).T.astype(BF16)
            e = ds_ref[rows] * sgate * (1.0 + n * (1.0 - sgate)) * gain_ref[...]
            zhat_ref[rows] = zhat
            e_ref[rows] = e
            both = [jnp.sum(e, axis=1, keepdims=True), jnp.sum(e * zhat, axis=1, keepdims=True)]
            sums[:, rows] = jnp.concatenate([as_row(both[0]), as_row(both[1])])

    return call(
        body,
        [
            ((block, length), BF16),
            ((length, block), F32),
            ((length, block), F32),
            ((1, length), F32),
            ((2, length), F32),
        ],
        [z, gain, d_s, *stats],
    )


def ungate(e, zhat, inv, sums, p, taps):
    length, block = e.shape
    kernel = taps.shape[0]
    half = kernel // 2
    tile = tile_width(block)

    count = len(sums)

    def body(e_ref, zhat_ref, inv_ref, p_ref, taps_ref, *refs):
        sum_refs, (dp_ref, dz_ref, padded) = refs[:count], refs[count:]
        for low in range(0, length, LANES):
            rows = slice(low, low + LANES)
            means = sum([ref[:, rows] for ref in sum_refs[1:]], sum_refs[0][:, rows])
            means = means / (block * count)
            mean, mean_z = as_column(means[:1]), as_column(means[1:])
            d_z = (e_ref[rows] - mean - zhat_ref[rows] * mean_z) * as_column(inv_ref[:, rows])
            dz_ref[rows] = d_z.astype(BF16)
        fill(
            padded,
            half,
            length,
            block,
            lambda low, col, size: dz_ref[low : low + LANES, col : col + size].astype(F32),
        )

        def write(start, chunk, cols, total):
            rows = pl.ds(start, chunk)
            first = p_ref[rows, cols]
            sig = jax.nn.sigmoid(p_ref[rows, slice(block + cols.start, block + cols.stop)])
            dp_ref[rows, cols] = (total * sig).astype(BF16)
            dp_ref[rows, slice(block + cols.start, block + cols.stop)] = (
                total * first * sig * (1.0 - sig)
            ).astype(BF16)

        convolve(
            padded, taps_ref, length, block, [2 * half - t for t in range(kernel)], write
        )

    return call(
        body,
        [((length, 2 * block), BF16), ((length, block), BF16)],
        [e, zhat, inv, p, taps, *sums],
        [pltpu.VMEM((block // tile, length + 2 * half, tile), F32)],
    )


def taps_gradient(d_z, y, kernel):
    length, block = y.shape
    half = kernel // 2
    tile = tile_width(block)
    group = 8

    def body(dz_ref, y_ref, out, dz_all, y_pad):
        for ref, padded in ((dz_ref, dz_all), (y_ref, y_pad)):
            fill(
                padded,
                half,
                length,
                block,
                lambda low, col, size, ref=ref: ref[low : low + LANES, col : col + size].astype(F32),
            )
        for i in range(block // tile):

            def step(j, sums, i=i):
                start = pl.multiple_of(j * group, group)
                value = dz_all[i, pl.ds(start + half, group)]
                return tuple(
                    total + value * y_pad[i, pl.ds(start + t, group)]
                    for t, total in enumerate(sums)
                )

            zero = jnp.zeros((group, tile), F32)
            sums = lax.fori_loop(0, length // group, step, (zero,) * kernel)
            out[:, i * tile : (i + 1) * tile] = jnp.concatenate(
                [jnp.sum(total, axis=0, keepdims=True) for total in sums]
            )

    pad = pltpu.VMEM((block // tile, length + 2 * half, tile), F32)
    return call(body, [((kernel, block), F32)], [d_z, y], [pad, pad])[0]


def gather_rows(value, axis, order):
    index = index_of(axis)
    value = value[(None,) * len(order)]
    for bit in order:
        other = swap(value, axis, bit)
        upper = (index // bit) % 2 == 1
        place = len(order) - bit.bit_length()
        value = jnp.concatenate(
            [jnp.where(upper, other, value), jnp.where(upper, value, other)], axis=place
        )
    return value.reshape((lax.axis_size(axis),) + value.shape[len(order) :])


def tree(value, axis, order):
    parts = {0: value}
    for bit in order:
        parts |= {offset ^ bit: swap(part, axis, bit) for offset, part in parts.items()}
    return parts


def rows_in_place(jobs, widths, axis, into=()):
    count, given = len(jobs), len(into)
    total = lax.axis_size(axis) * jobs[0][0].shape[0]

    def body(index, *refs):
        ins = refs[:count]
        outs = refs[count + given : count + given + len(widths)]
        wides, sem = refs[count + given + len(widths) : -1], refs[-1]
        copies = []
        for ref, wide, (_, offset, spans) in zip(ins, wides, jobs):
            share = ref.shape[0]
            wide[...] = ref[...].astype(F32)
            start = pl.multiple_of((index[0] ^ offset) * share, share)
            for which, low, high, place in spans:
                copy = pltpu.make_async_copy(
                    wide.at[:, low:high],
                    outs[which].at[pl.ds(start, share), place : place + high - low],
                    sem.at[len(copies)],
                )
                copy.start()
                copies.append(copy)
        for copy in copies:
            copy.wait()

    space = pl.BlockSpec(memory_space=pltpu.MemorySpace.VMEM)
    whole = pl.BlockSpec(memory_space=pl.ANY)
    return pl.pallas_call(
        body,
        out_shape=[jax.ShapeDtypeStruct((total, width), F32) for width in widths],
        in_specs=[pl.BlockSpec(memory_space=pltpu.MemorySpace.SMEM)]
        + [space] * count
        + [whole] * given,
        out_specs=[whole] * len(widths),
        scratch_shapes=[pltpu.VMEM(array.shape, F32) for array, _, _ in jobs]
        + [pltpu.SemaphoreType.DMA((sum(len(spans) for _, _, spans in jobs),))],
        input_output_aliases={count + 1 + j: j for j in range(given)},
        compiler_params=pltpu.CompilerParams(vmem_limit_bytes=56 * 1024 * 1024),
    )(index_of(axis).astype(jnp.int32).reshape(1), *[job[0] for job in jobs], *into)


def gather_both(left, right, out, near, far):
    share, middle = left.shape
    wide, width = 2 * middle, out.shape[1]
    cut = width // 2
    if share % 16 == 0 and cut % LANES == 0:
        one = tree(left, "dp", near)
        two = tree(jnp.concatenate([right, out[:, :cut]], axis=1), "dp", near)
        short = tree(out[:, cut:], "dp", far)
        spans = [(0, 0, middle, 0)], [
            (0, 0, wide - middle, middle),
            (1, middle, middle + cut, 0),
        ]
        jobs = [(part, o, spans[i]) for i, parts in enumerate((one, two)) for o, part in parts.items()]
        jobs += [(part, o, [(1, 0, cut, cut)]) for o, part in short.items()]
        first = [0] + near[:2]
        early = [job for job in jobs[: 2 * len(one)] if job[1] in first]
        early += [job for job in jobs[2 * len(one) :] if job[1] in (0, far[0])]
        rest = [job for job in jobs if not any(job is other for other in early)]
        into = rows_in_place(early, (wide, width), "dp")
        return rows_in_place(rest, (wide, width), "dp", into)
    glu = gather_rows(jnp.concatenate([left, right], axis=1), "dp", near).reshape(-1, wide)
    out = gather_rows(out, "dp", far).reshape(-1, width)
    return glu.astype(F32), out.astype(F32)


class Halving:
    def __init__(self, value, axis, order):
        self.axis, self.order = axis, list(order)
        self.left = sorted(order, reverse=True)
        self.value = value.reshape((2,) * len(order) + value.shape[1:])
        self.give = None

    def split(self):
        bit = self.order.pop(0)
        place = self.left.index(bit)
        self.left.remove(bit)
        mine = (index_of(self.axis) // bit) % 2
        self.bit = bit
        self.give = lax.dynamic_index_in_dim(self.value, 1 - mine, place, keepdims=False)
        self.give = self.give.astype(BF16)
        self.value = lax.dynamic_index_in_dim(self.value, mine, place, keepdims=False)

    def join(self):
        got = swap(self.give, self.axis, self.bit)
        self.value = self.value.astype(F32) + got.astype(F32)
        self.give = None


def together(items, *others):
    fixed = lax.optimization_barrier((tuple(item.give for item in items), others))
    for item, give in zip(items, fixed[0]):
        item.give = give
    return fixed[1]


def orders(size):
    bits = bits_of(size)
    return bits, bits[1:] + bits[:1]


def whole_step(frames, query, keys, values, norm_gain, conv_gain, w_glu, taps, w_out, cotangent):
    groups = lax.axis_size("tm")
    copies = lax.axis_size("dp")
    mine = index_of("tm")
    rows, width = frames.shape[1:]
    length = rows * groups
    block = width // groups
    share = block // copies
    tm_bits = bits_of(lax.axis_size("tm"))
    offsets = list(range(groups))
    near, far = orders(lax.axis_size("dp"))

    def columns(arr, owner, low=0):
        return lax.dynamic_slice_in_dim(arr, owner * block + low, block, arr.ndim - 1)

    norm_all = jnp.concatenate([columns(norm_gain[None], mine ^ o) for o in offsets])
    conv_own = columns(conv_gain[None], mine)
    taps_own = columns(taps, mine)

    def glu_columns(arr, owner):
        return jnp.concatenate([columns(arr, owner), columns(arr, owner, width)], axis=1)

    distant = [o for o in offsets if o > 1]
    if distant:
        place = index_of("dp") * share
        w_share = lax.dynamic_slice_in_dim(w_glu, place, share, 0)
        fetched = jnp.stack([swap(glu_columns(w_share, mine ^ o), "tm", o) for o in distant])

    def exchange(arrays):
        blocks = []
        for m in range(groups):
            piece = jnp.concatenate([columns(arr, mine ^ m) for arr in arrays])
            blocks.append(piece if m == 0 else swap(piece, "tm", m))
        return blocks

    blocks = exchange([query, keys, values])
    residual = exchange([frames])
    w_parts = {0: glu_columns(w_glu, mine), 1: swap(glu_columns(w_glu, mine ^ 1), "tm", 1)}

    w_far = {}
    if distant and share % 16 == 0:
        w_far = tree(fetched, "dp", near[::-1])
    elif distant:
        spread = gather_rows(fetched, "dp", near[::-1])
        for i, offset in enumerate(distant):
            w_parts[offset] = spread[:, i].reshape(block, 2 * block)

    mixed, stat_u = attend(mine, blocks, residual, width // HEADS)
    stats_u = tree(stat_u, "tm", tm_bits)
    parts = {0: mixed}
    for bit in reversed(tm_bits):
        parts |= {offset ^ bit: swap(part, "tm", bit) for offset, part in parts.items()}
    cot_all = gather_rows(cotangent[0], "tm", tm_bits[::-1]).reshape(length, width)
    d_s = lax.dot_general(cot_all, w_out, (((1,), (1,)), ((), ())), preferred_element_type=F32)

    last = parts[groups - 1]
    d_s, parts[groups - 1] = lax.optimization_barrier((d_s, last))
    u_all, p_own, y_rows, z_rows, stat_z = gate(
        [parts[o] for o in offsets],
        [stats_u[o] for o in offsets],
        norm_all,
        list(w_parts.values()),
        [w_far[o] for o in range(len(w_far))],
        taps_own,
    )
    stats_z = tree(stat_z, "tm", tm_bits)
    s_turned, zhat, e_rows, inv, sums = swish(z_rows, list(stats_z.values()), conv_own, d_s)
    contract = (((0,), (0,)), ((), ()))
    middle = width // 2
    out_term = jnp.dot(s_turned, cot_all, preferred_element_type=F32)
    out_term = out_term.reshape(copies, share, width)
    outs = [Halving(out_term[..., :middle], "dp", near), Halving(out_term[..., middle:], "dp", far)]
    steps = len(near)
    for item in outs:
        item.split()
    for item in outs:
        item.join()

    sums = list(tree(sums, "tm", tm_bits).values())
    d_p, d_z = ungate(e_rows, zhat, inv, sums, p_own, taps_own)
    if steps > 1:
        for item in outs:
            item.split()
        (d_p,) = together(outs, d_p)
        for item in outs:
            item.join()

    glu_term = lax.dot_general(u_all, d_p, contract, preferred_element_type=F32)
    glu_term = glu_term.reshape(groups, copies, share, 2 * block).transpose(1, 0, 2, 3)
    glus = [Halving(glu_term[..., :block], "dp", near), Halving(glu_term[..., block:], "dp", far)]
    for item in glus:
        item.split()
    d_z, y_rows = together(glus, d_z, y_rows)
    taps_sum = taps_gradient(d_z, y_rows, taps.shape[0])
    for item in glus:
        item.join()
    for i in range(1, steps):
        for item in glus:
            item.split()
        (taps_sum,) = together(glus[:1], taps_sum)
        if i + 1 < steps:
            for item in outs:
                item.split()
            together(glus[:1] + outs)
            for item in outs:
                item.join()
        taps_sum = taps_sum + swap(taps_sum, "dp", near[i - 1])
        for item in glus:
            item.join()

    pieces = []
    for item in glus:
        part = item.value.astype(BF16)
        got = jnp.stack([part[0]] + [swap(part[o], "tm", o) for o in offsets[1:]])
        if pieces:
            got, _ = lax.optimization_barrier((got, pieces[0]))
        ordered = [
            lax.dynamic_index_in_dim(got, mine ^ g, 0, keepdims=False) for g in range(groups)
        ]
        pieces.append(jnp.concatenate(ordered, axis=1))
    out_piece = jnp.concatenate([item.value.astype(BF16) for item in outs], axis=1)
    (taps_sum, pieces[1]) = lax.optimization_barrier((taps_sum, pieces[1]))
    taps_sum = taps_sum + swap(taps_sum, "dp", near[-1])
    glu_grad, out_grad = gather_both(*pieces, out_piece, near[::-1], far[::-1])
    return (glu_grad, taps_sum, out_grad)


def solution(mesh):
    return jax.shard_map(
        whole_step,
        mesh=mesh,
        in_specs=(
            P("dp", "tm", None),
            P("dp", "tm", None),
            P("dp", "tm", None),
            P("dp", "tm", None),
            P(),
            P(),
            P("tm", None),
            P(),
            P("tm", None),
            P("dp", "tm", None),
        ),
        out_specs=(P("tm", None), P(None, "tm"), P("tm", None)),
        check_vma=False,
    )
```

```python
import jax
import jax.numpy as jnp
from jax import lax
from jax.experimental import pallas as pl
from jax.experimental.pallas import tpu as pltpu
from jax.sharding import PartitionSpec as P


HEADS = 16
LANES = 128
ATTEND_ROWS = 512
F32 = jnp.float32
BF16 = jnp.bfloat16


def bits_of(size):
    return [1 << i for i in range(size.bit_length() - 1)]


def swap(value, axis, offset):
    size = lax.axis_size(axis)
    return lax.ppermute(value, axis, [(i, i ^ offset) for i in range(size)])


def index_of(axis):
    return lax.axis_index(axis).astype(jnp.uint32)


def tile_width(block):
    return LANES if block % LANES == 0 else block


def as_row(column):
    return jnp.broadcast_to(column, (column.shape[0], LANES)).T[:1]


def as_column(row):
    return jnp.broadcast_to(row, (LANES, row.shape[1])).T[:, :1]


def moments(value):
    mean = jnp.mean(value, axis=1, keepdims=True)
    centred = value - mean
    spread = jnp.sum(centred * centred, axis=1, keepdims=True)
    return centred, jnp.concatenate([as_row(mean), as_row(spread)])


def merge_moments(stats, rows, count):
    means = [stat[:1, rows] for stat in stats]
    mean = sum(means[1:], means[0]) / len(stats)
    spread = sum([stat[1:, rows] for stat in stats[1:]], stats[0][1:, rows])
    gaps = [(m - mean) * (m - mean) for m in means]
    spread = spread + count * sum(gaps[1:], gaps[0])
    return mean, lax.rsqrt(spread / (count * len(stats)) + 1e-05)


def call(body, outs, args, scratch=(), scalars=()):
    space = pl.BlockSpec(memory_space=pltpu.MemorySpace.VMEM)
    scalar = pl.BlockSpec(memory_space=pltpu.MemorySpace.SMEM)
    return pl.pallas_call(
        body,
        out_shape=[jax.ShapeDtypeStruct(shape, dtype) for shape, dtype in outs],
        in_specs=[scalar] * len(scalars) + [space] * len(args),
        out_specs=[space] * len(outs),
        scratch_shapes=list(scratch),
        compiler_params=pltpu.CompilerParams(vmem_limit_bytes=56 * 1024 * 1024),
    )(*scalars, *args)


def attend(mine, blocks, residual, head_dim):
    groups = len(blocks)
    rows, width = blocks[0].shape[1:]
    length = groups * rows
    scale = head_dim ** (-0.5)

    def body(index, *refs):
        parts, rest, (mixed, stat) = refs[:groups], refs[groups : 2 * groups], refs[2 * groups :]
        outs = []
        for low in range(0, width, head_dim):
            cols = slice(low, low + head_dim)
            q, k, v = [jnp.concatenate([part[i, :, cols] for part in parts]) for i in range(3)]
            heads = []
            for first in range(0, length, ATTEND_ROWS):
                scores = lax.dot_general(
                    q[first : first + ATTEND_ROWS],
                    k,
                    (((1,), (1,)), ((), ())),
                    preferred_element_type=F32,
                )
                scores = scores * scale
                expo = jnp.exp(scores - jnp.max(scores, axis=1, keepdims=True))
                total = jnp.sum(expo, axis=1, keepdims=True)
                summed = jnp.dot(expo.astype(BF16), v, preferred_element_type=F32)
                heads.append((summed / total).astype(BF16))
            outs.append(jnp.concatenate(heads))
        attention = jnp.concatenate(outs, axis=1)
        for m, part in enumerate(rest):
            start = pl.multiple_of((index[0] ^ m) * rows, rows)
            value = part[0].astype(F32) + attention[m * rows : (m + 1) * rows].astype(F32)
            centred, stat[:, pl.ds(start, rows)] = moments(value)
            mixed[pl.ds(start, rows), :] = centred.astype(BF16)

    return call(
        body, [((length, width), BF16), ((2, length), F32)],
        [*blocks, *residual],
        scalars=[mine.astype(jnp.int32).reshape(1)],
    )


def fill(padded, half, length, width, read):
    tile = tile_width(width)
    for i in range(width // tile):
        padded[i, :half] = jnp.zeros((half, tile), F32)
        padded[i, half + length :] = jnp.zeros((half, tile), F32)
        for low in range(0, length, LANES):
            padded[i, half + low : half + low + LANES] = read(low, i * tile, tile)


def convolve(padded, taps, length, width, places, write, chunk=128):
    tile = tile_width(width)
    for i in range(width // tile):
        cols = slice(i * tile, (i + 1) * tile)

        def step(j, carry, i=i, cols=cols):
            start = pl.multiple_of(j * chunk, chunk)
            total = jnp.zeros((chunk, tile), F32)
            for t, place in enumerate(places):
                total = total + taps[t : t + 1, cols] * padded[i, pl.ds(start + place, chunk)]
            write(start, chunk, cols, total)
            return carry

        lax.fori_loop(0, length // chunk, step, 0)


def gate(parts, stats, gain, w_near, w_far, taps):
    length, block = parts[0].shape
    count = len(parts)
    kernel = taps.shape[0]
    half = kernel // 2
    tile = tile_width(block)

    close, copies = len(w_near), len(w_far)

    def body(index, *refs):
        ins, ws, far = refs[:count], list(refs[count : count + close]), refs[count + close :]
        far, refs = far[:copies], far[copies:]
        stat_refs, refs = refs[:count], refs[count:]
        gain_ref, taps_ref, u_ref, p_ref, y_ref, z_ref, stat, padded = refs[:8]
        if copies:
            whole = refs[8]
            share = far[0].shape[1]
            for offset, ref in enumerate(far):
                start = pl.multiple_of((index[0] ^ offset) * share, share)
                for m in range(count - close):
                    whole[m, pl.ds(start, share), :] = ref[m]
            ws += [whole.at[m] for m in range(count - close)]
        for low in range(0, length, LANES):
            rows = slice(low, low + LANES)
            mean, inv = merge_moments(stat_refs, rows, block)
            shifts = [as_column(ref[:1, rows] - mean) for ref in stat_refs]
            inv = as_column(inv)
            p = jnp.zeros((LANES, 2 * block), F32)
            for m, (part, w) in enumerate(zip(ins, ws)):
                u = (part[rows].astype(F32) + shifts[m]) * inv * gain_ref[m : m + 1]
                u = u.astype(BF16)
                u_ref[rows, m * block : (m + 1) * block] = u
                p = p + jnp.dot(u, w[...], preferred_element_type=F32)
            p_ref[rows] = p
            y_ref[rows] = (p[:, :block] * jax.nn.sigmoid(p[:, block:])).astype(BF16)
        fill(
            padded,
            half,
            length,
            block,
            lambda low, col, size: y_ref[low : low + LANES, col : col + size].astype(F32),
        )

        def write(start, chunk, cols, total):
            z_ref[pl.ds(start, chunk), cols] = total

        convolve(padded, taps_ref, length, block, range(kernel), write)
        for low in range(0, length, LANES):
            rows = slice(low, low + LANES)
            stat[:, rows] = moments(z_ref[rows])[1]

    return call(
        body,
        [
            ((length, count * block), BF16),
            ((length, 2 * block), F32),
            ((length, block), BF16),
            ((length, block), F32),
            ((2, length), F32),
        ],
        [*parts, *w_near, *w_far, *stats, gain, taps],
        [pltpu.VMEM((block // tile, length + 2 * half, tile), F32)]
        + ([pltpu.VMEM((count - close, block, 2 * block), BF16)] if copies else []),
        scalars=[index_of("dp").astype(jnp.int32).reshape(1)],
    )


def swish(z, stats, gain, d_s):
    length, block = z.shape
    count = len(stats)

    def body(z_ref, gain_ref, ds_ref, *refs):
        stat_refs, (s_ref, zhat_ref, e_ref, inv_ref, sums) = refs[:count], refs[count:]
        for low in range(0, length, LANES):
            rows = slice(low, low + LANES)
            mean, inv = merge_moments(stat_refs, rows, block)
            inv_ref[:, rows] = inv
            zhat = (z_ref[rows] - as_column(mean)) * as_column(inv)
            n = zhat * gain_ref[...]
            sgate = jax.nn.sigmoid(n)
            s_ref[:, rows] = (n * sgate).T.astype(BF16)
            e = ds_ref[rows] * sgate * (1.0 + n * (1.0 - sgate)) * gain_ref[...]
            zhat_ref[rows] = zhat
            e_ref[rows] = e
            both = [jnp.sum(e, axis=1, keepdims=True), jnp.sum(e * zhat, axis=1, keepdims=True)]
            sums[:, rows] = jnp.concatenate([as_row(both[0]), as_row(both[1])])

    return call(
        body,
        [
            ((block, length), BF16),
            ((length, block), F32),
            ((length, block), F32),
            ((1, length), F32),
            ((2, length), F32),
        ],
        [z, gain, d_s, *stats],
    )


def ungate(e, zhat, inv, sums, p, taps):
    length, block = e.shape
    kernel = taps.shape[0]
    half = kernel // 2
    tile = tile_width(block)

    count = len(sums)

    def body(e_ref, zhat_ref, inv_ref, p_ref, taps_ref, *refs):
        sum_refs, (dp_ref, dz_ref, padded) = refs[:count], refs[count:]
        for low in range(0, length, LANES):
            rows = slice(low, low + LANES)
            means = sum([ref[:, rows] for ref in sum_refs[1:]], sum_refs[0][:, rows])
            means = means / (block * count)
            mean, mean_z = as_column(means[:1]), as_column(means[1:])
            d_z = (e_ref[rows] - mean - zhat_ref[rows] * mean_z) * as_column(inv_ref[:, rows])
            dz_ref[rows] = d_z.astype(BF16)
        fill(
            padded,
            half,
            length,
            block,
            lambda low, col, size: dz_ref[low : low + LANES, col : col + size].astype(F32),
        )

        def write(start, chunk, cols, total):
            rows = pl.ds(start, chunk)
            first = p_ref[rows, cols]
            sig = jax.nn.sigmoid(p_ref[rows, slice(block + cols.start, block + cols.stop)])
            dp_ref[rows, cols] = (total * sig).astype(BF16)
            dp_ref[rows, slice(block + cols.start, block + cols.stop)] = (
                total * first * sig * (1.0 - sig)
            ).astype(BF16)

        convolve(
            padded, taps_ref, length, block, [2 * half - t for t in range(kernel)], write
        )

    return call(
        body,
        [((length, 2 * block), BF16), ((length, block), BF16)],
        [e, zhat, inv, p, taps, *sums],
        [pltpu.VMEM((block // tile, length + 2 * half, tile), F32)],
    )


def taps_gradient(d_z, y, kernel):
    length, block = y.shape
    half = kernel // 2
    tile = tile_width(block)
    group = 8

    def body(dz_ref, y_ref, out, dz_all, y_pad):
        for ref, padded in ((dz_ref, dz_all), (y_ref, y_pad)):
            fill(
                padded,
                half,
                length,
                block,
                lambda low, col, size, ref=ref: ref[low : low + LANES, col : col + size].astype(F32),
            )
        for i in range(block // tile):

            def step(j, sums, i=i):
                start = pl.multiple_of(j * group, group)
                value = dz_all[i, pl.ds(start + half, group)]
                return tuple(
                    total + value * y_pad[i, pl.ds(start + t, group)]
                    for t, total in enumerate(sums)
                )

            zero = jnp.zeros((group, tile), F32)
            sums = lax.fori_loop(0, length // group, step, (zero,) * kernel)
            out[:, i * tile : (i + 1) * tile] = jnp.concatenate(
                [jnp.sum(total, axis=0, keepdims=True) for total in sums]
            )

    pad = pltpu.VMEM((block // tile, length + 2 * half, tile), F32)
    return call(body, [((kernel, block), F32)], [d_z, y], [pad, pad])[0]


def gather_rows(value, axis, order):
    index = index_of(axis)
    value = value[(None,) * len(order)]
    for bit in order:
        other = swap(value, axis, bit)
        upper = (index // bit) % 2 == 1
        place = len(order) - bit.bit_length()
        value = jnp.concatenate(
            [jnp.where(upper, other, value), jnp.where(upper, value, other)], axis=place
        )
    return value.reshape((lax.axis_size(axis),) + value.shape[len(order) :])


def tree(value, axis, order):
    parts = {0: value}
    for bit in order:
        parts |= {offset ^ bit: swap(part, axis, bit) for offset, part in parts.items()}
    return parts


def rows_in_place(jobs, widths, axis, into=()):
    count, given = len(jobs), len(into)
    total = lax.axis_size(axis) * jobs[0][0].shape[0]

    def body(index, *refs):
        ins = refs[:count]
        outs = refs[count + given : count + given + len(widths)]
        scratch = refs[count + given + len(widths) :]
        held, wides, (fetched, sem) = scratch[:count], scratch[count:-2], scratch[-2:]
        fetches = [
            pltpu.make_async_copy(ref, block, fetched.at[i])
            for i, (ref, block) in enumerate(zip(ins, held))
        ]
        for fetch in fetches:
            fetch.start()
        copies = []
        for fetch, ref, wide, (_, offset, spans) in zip(fetches, held, wides, jobs):
            share = ref.shape[0]
            fetch.wait()
            wide[...] = ref[...].astype(F32)
            start = pl.multiple_of((index[0] ^ offset) * share, share)
            for which, low, high, place in spans:
                copy = pltpu.make_async_copy(
                    wide.at[:, low:high],
                    outs[which].at[pl.ds(start, share), place : place + high - low],
                    sem.at[len(copies)],
                )
                copy.start()
                copies.append(copy)
        for copy in copies:
            copy.wait()

    whole = pl.BlockSpec(memory_space=pl.ANY)
    return pl.pallas_call(
        body,
        out_shape=[jax.ShapeDtypeStruct((total, width), F32) for width in widths],
        in_specs=[pl.BlockSpec(memory_space=pltpu.MemorySpace.SMEM)]
        + [whole] * (count + given),
        out_specs=[whole] * len(widths),
        scratch_shapes=[pltpu.VMEM(array.shape, BF16) for array, _, _ in jobs]
        + [pltpu.VMEM(array.shape, F32) for array, _, _ in jobs]
        + [pltpu.SemaphoreType.DMA((count,))]
        + [pltpu.SemaphoreType.DMA((sum(len(spans) for _, _, spans in jobs),))],
        input_output_aliases={count + 1 + j: j for j in range(given)},
        compiler_params=pltpu.CompilerParams(vmem_limit_bytes=56 * 1024 * 1024),
    )(index_of(axis).astype(jnp.int32).reshape(1), *[job[0] for job in jobs], *into)


def gather_both(left, right, out, near, far):
    share, middle = left.shape
    wide, width = 2 * middle, out.shape[1]
    cut = width // 2
    if share % 16 == 0 and cut % LANES == 0:
        one = tree(left, "dp", near)
        two = tree(jnp.concatenate([right, out[:, :cut]], axis=1), "dp", near)
        short = tree(out[:, cut:], "dp", far)
        spans = [(0, 0, middle, 0)], [
            (0, 0, wide - middle, middle),
            (1, middle, middle + cut, 0),
        ]
        jobs = [(part, o, spans[i]) for i, parts in enumerate((one, two)) for o, part in parts.items()]
        jobs += [(part, o, [(1, 0, cut, cut)]) for o, part in short.items()]
        first = [0] + near[:2]
        early = [job for job in jobs[: 2 * len(one)] if job[1] in first]
        early += [job for job in jobs[2 * len(one) :] if job[1] in (0, far[0])]
        rest = [job for job in jobs if not any(job is other for other in early)]
        into = rows_in_place(early, (wide, width), "dp")
        return rows_in_place(rest, (wide, width), "dp", into)
    glu = gather_rows(jnp.concatenate([left, right], axis=1), "dp", near).reshape(-1, wide)
    out = gather_rows(out, "dp", far).reshape(-1, width)
    return glu.astype(F32), out.astype(F32)


class Halving:
    def __init__(self, value, axis, order):
        self.axis, self.order = axis, list(order)
        self.left = sorted(order, reverse=True)
        self.value = value.reshape((2,) * len(order) + value.shape[1:])
        self.give = None

    def split(self):
        bit = self.order.pop(0)
        place = self.left.index(bit)
        self.left.remove(bit)
        mine = (index_of(self.axis) // bit) % 2
        self.bit = bit
        self.give = lax.dynamic_index_in_dim(self.value, 1 - mine, place, keepdims=False)
        self.give = self.give.astype(BF16)
        self.value = lax.dynamic_index_in_dim(self.value, mine, place, keepdims=False)

    def join(self):
        got = swap(self.give, self.axis, self.bit)
        self.value = self.value.astype(F32) + got.astype(F32)
        self.give = None


def together(items, *others):
    fixed = lax.optimization_barrier((tuple(item.give for item in items), others))
    for item, give in zip(items, fixed[0]):
        item.give = give
    return fixed[1]


def orders(size):
    bits = bits_of(size)
    return bits, bits[1:] + bits[:1]


def whole_step(frames, query, keys, values, norm_gain, conv_gain, w_glu, taps, w_out, cotangent):
    groups = lax.axis_size("tm")
    copies = lax.axis_size("dp")
    mine = index_of("tm")
    rows, width = frames.shape[1:]
    length = rows * groups
    block = width // groups
    share = block // copies
    tm_bits = bits_of(lax.axis_size("tm"))
    offsets = list(range(groups))
    near, far = orders(lax.axis_size("dp"))

    def columns(arr, owner, low=0):
        return lax.dynamic_slice_in_dim(arr, owner * block + low, block, arr.ndim - 1)

    norm_all = jnp.concatenate([columns(norm_gain[None], mine ^ o) for o in offsets])
    conv_own = columns(conv_gain[None], mine)
    taps_own = columns(taps, mine)

    def glu_columns(arr, owner):
        return jnp.concatenate([columns(arr, owner), columns(arr, owner, width)], axis=1)

    distant = [o for o in offsets if o > 1]
    if distant:
        place = index_of("dp") * share
        w_share = lax.dynamic_slice_in_dim(w_glu, place, share, 0)
        fetched = jnp.stack([swap(glu_columns(w_share, mine ^ o), "tm", o) for o in distant])

    def exchange(arrays):
        blocks = []
        for m in range(groups):
            piece = jnp.concatenate([columns(arr, mine ^ m) for arr in arrays])
            blocks.append(piece if m == 0 else swap(piece, "tm", m))
        return blocks

    blocks = exchange([query, keys, values])
    residual = exchange([frames])
    w_parts = {0: glu_columns(w_glu, mine), 1: swap(glu_columns(w_glu, mine ^ 1), "tm", 1)}

    w_far = {}
    if distant and share % 16 == 0:
        w_far = tree(fetched, "dp", near[::-1])
    elif distant:
        spread = gather_rows(fetched, "dp", near[::-1])
        for i, offset in enumerate(distant):
            w_parts[offset] = spread[:, i].reshape(block, 2 * block)

    mixed, stat_u = attend(mine, blocks, residual, width // HEADS)
    stats_u = tree(stat_u, "tm", tm_bits)
    parts = {0: mixed}
    for bit in reversed(tm_bits):
        parts |= {offset ^ bit: swap(part, "tm", bit) for offset, part in parts.items()}
    cot_all = gather_rows(cotangent[0], "tm", tm_bits[::-1]).reshape(length, width)
    d_s = lax.dot_general(cot_all, w_out, (((1,), (1,)), ((), ())), preferred_element_type=F32)

    last = parts[groups - 1]
    d_s, parts[groups - 1] = lax.optimization_barrier((d_s, last))
    u_all, p_own, y_rows, z_rows, stat_z = gate(
        [parts[o] for o in offsets],
        [stats_u[o] for o in offsets],
        norm_all,
        list(w_parts.values()),
        [w_far[o] for o in range(len(w_far))],
        taps_own,
    )
    stats_z = tree(stat_z, "tm", tm_bits)
    s_turned, zhat, e_rows, inv, sums = swish(z_rows, list(stats_z.values()), conv_own, d_s)
    contract = (((0,), (0,)), ((), ()))
    middle = width // 2
    out_term = jnp.dot(s_turned, cot_all, preferred_element_type=F32)
    out_term = out_term.reshape(copies, share, width)
    outs = [Halving(out_term[..., :middle], "dp", near), Halving(out_term[..., middle:], "dp", far)]
    steps = len(near)
    for item in outs:
        item.split()
    for item in outs:
        item.join()

    sums = list(tree(sums, "tm", tm_bits).values())
    d_p, d_z = ungate(e_rows, zhat, inv, sums, p_own, taps_own)
    if steps > 1:
        for item in outs:
            item.split()
        (d_p,) = together(outs, d_p)
        for item in outs:
            item.join()

    glu_term = lax.dot_general(u_all, d_p, contract, preferred_element_type=F32)
    glu_term = glu_term.reshape(groups, copies, share, 2 * block).transpose(1, 0, 2, 3)
    glus = [Halving(glu_term[..., :block], "dp", near), Halving(glu_term[..., block:], "dp", far)]
    for item in glus:
        item.split()
    d_z, y_rows = together(glus, d_z, y_rows)
    taps_sum = taps_gradient(d_z, y_rows, taps.shape[0])
    for item in glus:
        item.join()
    for i in range(1, steps):
        for item in glus:
            item.split()
        (taps_sum,) = together(glus[:1], taps_sum)
        if i + 1 < steps:
            for item in outs:
                item.split()
            together(glus[:1] + outs)
            for item in outs:
                item.join()
        taps_sum = taps_sum + swap(taps_sum, "dp", near[i - 1])
        for item in glus:
            item.join()

    pieces = []
    for item in glus:
        part = item.value.astype(BF16)
        got = jnp.stack([part[0]] + [swap(part[o], "tm", o) for o in offsets[1:]])
        if pieces:
            got, _ = lax.optimization_barrier((got, pieces[0]))
        ordered = [
            lax.dynamic_index_in_dim(got, mine ^ g, 0, keepdims=False) for g in range(groups)
        ]
        pieces.append(jnp.concatenate(ordered, axis=1))
    out_piece = jnp.concatenate([item.value.astype(BF16) for item in outs], axis=1)
    (taps_sum, pieces[1]) = lax.optimization_barrier((taps_sum, pieces[1]))
    taps_sum = taps_sum + swap(taps_sum, "dp", near[-1])
    glu_grad, out_grad = gather_both(*pieces, out_piece, near[::-1], far[::-1])
    return (glu_grad, taps_sum, out_grad)


def solution(mesh):
    return jax.shard_map(
        whole_step,
        mesh=mesh,
        in_specs=(
            P("dp", "tm", None),
            P("dp", "tm", None),
            P("dp", "tm", None),
            P("dp", "tm", None),
            P(),
            P(),
            P("tm", None),
            P(),
            P("tm", None),
            P("dp", "tm", None),
        ),
        out_specs=(P("tm", None), P(None, "tm"), P("tm", None)),
        check_vma=False,
    )
```
